512 devices in a mesh: blk: 64 (over z, x_lo, core), rep: 8 (over y, x_hi).
Axes of the slice: x: 4 (x_hi: 2, x_lo: 2; x = x_hi * 2 + x_lo), y: 4, z: 16, core: 2. Of those that a mesh axis runs over, the one named last changes fastest.
Arguments:
- features: bfloat16 [65536, 256], P(('blk', 'rep')), may hold values from -6 to 6
- out_grad: bfloat16 [65536, 256], P('blk'), may hold values from -4 to 4
- weight: bfloat16 [256, 256], replicated, may hold values from -0.375 to 0.375
- block_words: int32 [64, 64, 8, 16, 128], P('blk', 'rep'), may hold values from 0 to 255
- block_coords: int32 [64, 64, 2, 8], P('blk', 'rep'), may hold values from 0 to 7, as said below
- block_counts: int32 [64, 64], P('blk', 'rep'), may hold values from 1 to 8, as said below
- degrees: int32 [65536], P('blk'), may hold values from 1 to 127
Outputs:
- input_grad: bfloat16 [65536, 256], P(('blk', 'rep'))
- weight_grad: float32 [256, 256], replicated
The draws below stay inside these ranges and needn't reach their ends.
Inputs may be any that keep to these rules, and one draw needn't show every extreme that they name: `block_coords`: within one slab pair the 8 slots name distinct pairs of row block and column block. `block_counts`: the 8 slab pairs of one device include one in which all 8 slots are live.
All inputs are finite; a program needn't handle non-finite values.
Results may differ from the reference program's by a relative error of at most 0.015.
Values may be sent and summed in bfloat16 or wider, within the bound.
A program may use at most 64 MiB of HBM per device.

```python
import math
import jax
import jax.numpy as jnp
from jax import lax

F = 256
SLABS = 64
STEPS = 8
RB = 8
BMAX = 8
NODES = 65536


def draw_block_coords(key, part):
    cells = RB * RB
    scores = jax.random.randint(key, (SLABS, SLABS, cells), 0, 65536) * cells + jnp.arange(cells, dtype=jnp.int32)
    order = jnp.argsort(scores, axis=-1)[:, :, :BMAX].astype(jnp.int32)
    return jnp.stack([order // RB, order % RB], axis=2).astype(jnp.int32)


def draw_block_counts(key, part):
    key_one, key_two = jax.random.split(key)
    drawn = jax.random.randint(key_one, (SLABS, SLABS), 0, BMAX)
    counts = 1 + drawn * drawn // BMAX
    groups = SLABS // STEPS
    position = jax.random.randint(key_two, (SLABS, groups), 0, STEPS)
    chosen = jnp.arange(groups, dtype=jnp.int32)[None, :] * STEPS + position
    full_pair = jnp.any(jnp.arange(SLABS, dtype=jnp.int32)[None, None, :] == chosen[:, :, None], axis=1)
    return jnp.where(full_pair, BMAX, counts).astype(jnp.int32)


def draw_degrees(key, part):
    key_one, key_two = jax.random.split(key)
    exponent = jax.random.randint(key_one, (NODES,), 0, 7)
    base = jnp.left_shift(jnp.ones((NODES,), jnp.int32), exponent)
    extra = jax.random.randint(key_two, (NODES,), 0, base)
    return (base + extra).astype(jnp.int32)


def with_ends(entries, rng, low, top_value):
    shape = entries.shape
    index_at = [jax.random.randint(jax.random.fold_in(rng, axis), (), 0, shape[axis]) for axis in range(len(shape))]
    entries = entries.at[tuple(index_at)].set(low)
    longest = shape.index(max(shape))
    index_at[longest] = (index_at[longest] + 1) % shape[longest]
    return entries.at[tuple(index_at)].set(top_value)


def steps_of(key, shape, cuts, least, high):
    factor_of = 1.0
    for dim, parts in cuts:
        heights = jax.random.uniform(jax.random.fold_in(jax.random.fold_in(key, 6), dim), (parts,), jnp.float32, least / len(cuts), high / len(cuts))
        factor_of = factor_of * jnp.repeat(jnp.exp(heights), shape[dim] // parts).reshape((-1,) + (1,) * (len(shape) - 1 - dim))
    return factor_of


def noise(stream_key, dims, spread, reach, cuts=(), kind=jnp.bfloat16):
    loudness = steps_of(stream_key, dims, cuts, -0.22, 0.18) if cuts else 1.0
    values = jax.random.normal(stream_key, dims, jnp.float32) * spread * loudness
    return jnp.minimum(jnp.maximum(values, -reach), reach).astype(kind)


def setup_inputs(seed: int = 0) -> dict:
    keys = jax.random.split(jax.random.key(seed), 8)
    return {
        "features": noise(keys[0], (NODES, F), 1.0, 6.0, ((0, 512),)),
        "out_grad": noise(keys[1], (NODES, F), 0.5, 4.0, ((0, 64),)),
        "weight": noise(keys[2], (F, F), F ** -0.5, 0.375),
        "block_words": with_ends(jax.random.randint(keys[3], (SLABS, SLABS, BMAX, 16, 128), 0, 256), jax.random.fold_in(keys[3], 1), 0, 255).astype(jnp.int32),
        "block_coords": draw_block_coords(jax.random.fold_in(keys[7], 71), 0),
        "block_counts": draw_block_counts(jax.random.fold_in(keys[7], 71), 0),
        "degrees": draw_degrees(jax.random.fold_in(keys[7], 71), 0),
    }


def unpack_block(slot_words):
    shifts = jnp.arange(8, dtype=jnp.int32)
    bit_values = jnp.bitwise_and(jnp.right_shift(slot_words[:, :, None, :], shifts[None, None, :, None]), 1)
    return bit_values.reshape(slot_words.shape[0], 128, 128).astype(jnp.float32)

def reference(features, out_grad, weight, block_words, block_coords, block_counts, degrees):
    inverse_root = lax.rsqrt(degrees.astype(jnp.float32))
    scaled = (out_grad.astype(jnp.float32) * inverse_root[:, None]).astype(jnp.bfloat16)
    slabs = scaled.reshape(SLABS, RB, 128, F)
    column_ids = jnp.arange(RB, dtype=jnp.int32)
    slot_ids = jnp.arange(BMAX, dtype=jnp.int32)

    def one_target(target):

        def one_pair(accumulated, offset):
            source = (target + offset) % SLABS
            coords = block_coords[target, offset]
            live_count = block_counts[target, offset]
            picked = jnp.take(slabs[source], coords[0], axis=0).astype(jnp.float32)
            transposed = unpack_block(block_words[target, offset])
            contrib = jnp.einsum('bvu,buf->bvf', transposed, picked)
            live_slots = slot_ids < live_count
            placement = ((coords[1][:, None] == column_ids[None, :]) & live_slots[:, None]).astype(jnp.float32)
            return (accumulated + jnp.einsum('bc,bvf->cvf', placement, contrib), None)
        accumulated, _ = lax.scan(one_pair, jnp.zeros((RB, 128, F), jnp.float32), jnp.arange(SLABS, dtype=jnp.int32))
        return accumulated
    summed = lax.map(one_target, jnp.arange(SLABS, dtype=jnp.int32)).reshape(NODES, F)
    aggregated = (summed * inverse_root[:, None]).astype(jnp.bfloat16)
    input_grad = jnp.dot(aggregated, weight.T, preferred_element_type=jnp.float32).astype(jnp.bfloat16)
    weight_grad = jnp.dot(features.T, aggregated, preferred_element_type=jnp.float32) * (1.0 / math.sqrt(NODES))
    return (input_grad, weight_grad)
```

```python
import math

import jax
import jax.numpy as jnp
from jax import lax
from jax.sharding import PartitionSpec as P


def from_behind(block, axis, distance):
    devices = range(lax.axis_size(axis))
    route = [((i - distance) % len(devices), i) for i in devices]
    return lax.ppermute(block, axis, route)


def scatter_sum(flat, axis):
    size = lax.axis_size(axis)
    pieces = lax.all_to_all(flat.reshape(size, -1), axis, 0, 0, tiled=False)
    return pieces.sum(0)


def gather_all(piece, axis):
    size = lax.axis_size(axis)
    copies = jnp.broadcast_to(piece[None], (size,) + piece.shape)
    return lax.all_to_all(copies, axis, 0, 0, tiled=False).reshape(-1)


def all_reduce_by_exchange(term):
    flat = scatter_sum(scatter_sum(term.reshape(-1), "rep"), "blk")
    return gather_all(gather_all(flat, "blk"), "rep").reshape(term.shape)


def unpack_block(slot_words):
    shifts = jnp.arange(8, dtype=jnp.int32)
    bit_values = jnp.bitwise_and(
        jnp.right_shift(slot_words[:, :, None, :], shifts[None, None, :, None]), 1
    )
    return bit_values.reshape(slot_words.shape[0], 128, 128).astype(jnp.bfloat16)


def per_device(features, out_grad, weight, block_words, block_coords, block_counts, degrees):
    slab_rows, width = out_grad.shape
    row_blocks = slab_rows // 128
    group_size = lax.axis_size("rep")
    step_count = lax.axis_size("blk") // group_size
    rep_index = lax.axis_index("rep")
    inverse_root = lax.rsqrt(degrees.astype(jnp.float32))
    scaled = (out_grad.astype(jnp.float32) * inverse_root[:, None]).astype(jnp.bfloat16)
    column_ids = jnp.arange(row_blocks, dtype=jnp.int32)
    slot_total = block_words.shape[2]
    slot_ids = jnp.arange(slot_total, dtype=jnp.int32)

    def add_slot(accumulated, source_slab, slot_index):
        slot_words = lax.dynamic_index_in_dim(block_words[0], slot_index, 0, keepdims=False)
        coords = lax.dynamic_index_in_dim(block_coords[0], slot_index, 0, keepdims=False)
        live_count = lax.dynamic_index_in_dim(block_counts[0], slot_index, 0, keepdims=False)
        picked = jnp.take(source_slab.reshape(row_blocks, 128, width), coords[0], axis=0)
        transposed = unpack_block(slot_words)
        contrib = jnp.einsum("bvu,buf->bvf", transposed, picked, preferred_element_type=jnp.float32)
        live_slots = slot_ids < live_count
        placement = ((coords[1][:, None] == column_ids[None, :]) & live_slots[:, None]).astype(
            jnp.float32
        )
        return accumulated + jnp.einsum("bc,bvf->cvf", placement, contrib)

    empty = jnp.zeros((row_blocks, 128, width), jnp.float32)
    current = scaled
    for bit in range(group_size.bit_length() - 1):
        shifted = from_behind(current, "blk", -(1 << bit) * step_count)
        current = jnp.where(
            jnp.bitwise_and(jnp.right_shift(rep_index, bit), 1) == 1, shifted, current
        )
    accumulated = add_slot(empty, current, 0)

    def advance(step_index, state_tuple):
        current, accumulated = state_tuple
        current = from_behind(current, "blk", -1)
        return (current, add_slot(accumulated, current, step_index))

    current, accumulated = lax.fori_loop(1, step_count, advance, (current, accumulated))
    partial_sums = accumulated.reshape(slab_rows, width)
    share_rows = slab_rows // group_size
    share_root = lax.dynamic_slice_in_dim(inverse_root, rep_index * share_rows, share_rows, 0)
    exchanged = lax.all_to_all(
        partial_sums.reshape(group_size, share_rows, width), "rep", 0, 0, tiled=False
    )
    own_sums = exchanged.sum(0)
    aggregated = (own_sums * share_root[:, None]).astype(jnp.bfloat16)
    input_grad = lax.dot_general(
        aggregated, weight, (((1,), (1,)), ((), ())), preferred_element_type=jnp.float32
    ).astype(jnp.bfloat16)
    weight_term = lax.dot_general(
        features, aggregated, (((0,), (0,)), ((), ())), preferred_element_type=jnp.float32
    )
    node_total = slab_rows * lax.axis_size("blk")
    weight_grad = all_reduce_by_exchange(weight_term) * (1.0 / math.sqrt(node_total))
    return (input_grad, weight_grad)


def solution(mesh):
    return jax.shard_map(
        per_device,
        mesh=mesh,
        in_specs=(
            P(("blk", "rep"), None),
            P("blk", None),
            P(),
            P("blk", "rep", None, None, None),
            P("blk", "rep", None, None),
            P("blk", "rep"),
            P("blk"),
        ),
        out_specs=(P(("blk", "rep"), None), P()),
        check_vma=False,
    )
```

```python
import functools
import math

import jax
import jax.numpy as jnp
from jax import lax
from jax.experimental import pallas as pl
from jax.experimental.pallas import tpu as pltpu
from jax.sharding import PartitionSpec as P

CHUNKS = 4
MESH_ID = pl.DeviceIdType.MESH


def gather_kernel(steps, blocks, slab_ref, out_ref, send_sem, recv_sem, local_sem):
    me = lax.axis_index("blk")
    rep = lax.axis_index("rep")
    rows = slab_ref.shape[0] // CHUNKS
    far_to = lax.rem(me - steps * rep + blocks * steps, blocks)
    far_from = lax.rem(me + steps * rep, blocks)
    left = lax.rem(me + blocks - 1, blocks)
    right = lax.rem(me + 1, blocks)
    remote_first = rep != 0

    barrier = pltpu.get_barrier_semaphore()
    for partner in (left, right):
        pl.semaphore_signal(barrier, inc=1, device_id=(partner, rep), device_id_type=MESH_ID)

    @pl.when(remote_first)
    def _():
        for partner in (far_to, far_from):
            pl.semaphore_signal(barrier, inc=1, device_id=(partner, rep), device_id_type=MESH_ID)
        pl.semaphore_wait(barrier, 4)

    @pl.when(jnp.logical_not(remote_first))
    def _():
        pl.semaphore_wait(barrier, 2)

    def part(c):
        return pl.ds(c * rows, rows)

    def forward(s, c, target):
        src = slab_ref.at[part(c)] if s == 0 else out_ref.at[s - 1, part(c)]
        return pltpu.make_async_remote_copy(
            src_ref=src,
            dst_ref=out_ref.at[s, part(c)],
            send_sem=send_sem.at[s, c],
            recv_sem=recv_sem.at[s, c],
            device_id=(target, rep),
            device_id_type=MESH_ID,
        )

    @pl.when(remote_first)
    def _():
        for c in range(CHUNKS):
            forward(0, c, far_to).start()

    @pl.when(jnp.logical_not(remote_first))
    def _():
        for c in range(CHUNKS):
            local = pltpu.make_async_copy(slab_ref.at[part(c)], out_ref.at[0, part(c)], local_sem.at[c])
            local.start()
        for c in range(CHUNKS):
            pltpu.make_async_copy(slab_ref.at[part(c)], out_ref.at[0, part(c)], local_sem.at[c]).wait()

    for s in range(1, steps):
        for c in range(CHUNKS):
            if s == 1:
                @pl.when(remote_first)
                def _():
                    forward(0, c, far_to).wait_recv()
            else:
                forward(s - 1, c, left).wait_recv()
            forward(s, c, left).start()

    for c in range(CHUNKS):
        forward(steps - 1, c, left).wait_recv()

    @pl.when(remote_first)
    def _():
        for c in range(CHUNKS):
            forward(0, c, far_to).wait_send()

    for s in range(1, steps):
        for c in range(CHUNKS):
            forward(s, c, left).wait_send()


def gather_sources(scaled, steps, blocks):
    slab_rows, width = scaled.shape
    return pl.pallas_call(
        functools.partial(gather_kernel, steps, blocks),
        out_shape=jax.ShapeDtypeStruct((steps, slab_rows, width), scaled.dtype),
        in_specs=[pl.BlockSpec(memory_space=pl.ANY)],
        out_specs=pl.BlockSpec(memory_space=pl.ANY),
        scratch_shapes=[
            pltpu.SemaphoreType.DMA((steps, CHUNKS)),
            pltpu.SemaphoreType.DMA((steps, CHUNKS)),
            pltpu.SemaphoreType.DMA((CHUNKS,)),
        ],
        compiler_params=pltpu.CompilerParams(collective_id=0, has_side_effects=True),
    )(scaled)


def scatter_sum(flat, axis):
    size = lax.axis_size(axis)
    pieces = lax.all_to_all(flat.reshape(size, -1), axis, 0, 0, tiled=False)
    return pieces.sum(0)


def gather_all(piece, axis):
    size = lax.axis_size(axis)
    copies = jnp.broadcast_to(piece[None], (size,) + piece.shape)
    return lax.all_to_all(copies, axis, 0, 0, tiled=False).reshape(-1)


def all_reduce_by_exchange(term):
    flat = scatter_sum(scatter_sum(term.reshape(-1), "rep"), "blk")
    return gather_all(gather_all(flat, "blk"), "rep").reshape(term.shape)


def unpack_blocks(words):
    shifts = jnp.arange(8, dtype=jnp.int32)
    bit_values = jnp.bitwise_and(
        jnp.right_shift(words[..., :, None, :], shifts[:, None]), 1
    )
    return bit_values.reshape(words.shape[:-2] + (128, 128)).astype(jnp.bfloat16)


def per_device(features, out_grad, weight, block_words, block_coords, block_counts, degrees):
    slab_rows, width = out_grad.shape
    row_blocks = slab_rows // 128
    group_size = lax.axis_size("rep")
    blocks = lax.axis_size("blk")
    step_count = blocks // group_size
    rep_index = lax.axis_index("rep")
    inverse_root = lax.rsqrt(degrees.astype(jnp.float32))
    scaled = (out_grad.astype(jnp.float32) * inverse_root[:, None]).astype(jnp.bfloat16)

    sources = gather_sources(scaled, step_count, blocks).reshape(
        step_count, row_blocks, 128, width
    )
    coords = block_coords[0]
    slot_total = coords.shape[-1]
    picked = jnp.take_along_axis(sources, coords[:, 0, :, None, None], axis=1)
    transposed = unpack_blocks(block_words[0])
    contrib = jnp.einsum(
        "skvu,skuf->skvf", transposed, picked, preferred_element_type=jnp.float32
    )
    live = jnp.arange(slot_total, dtype=jnp.int32)[None, :] < block_counts[0][:, None]
    column_ids = jnp.arange(row_blocks, dtype=jnp.int32)
    placement = (
        (coords[:, 1, :, None] == column_ids[None, None, :]) & live[:, :, None]
    ).astype(jnp.float32)
    accumulated = jnp.einsum("skc,skvf->cvf", placement, contrib)

    partial_sums = accumulated.reshape(slab_rows, width)
    share_rows = slab_rows // group_size
    share_root = lax.dynamic_slice_in_dim(inverse_root, rep_index * share_rows, share_rows, 0)
    exchanged = lax.all_to_all(
        partial_sums.reshape(group_size, share_rows, width), "rep", 0, 0, tiled=False
    )
    own_sums = exchanged.sum(0)
    aggregated = (own_sums * share_root[:, None]).astype(jnp.bfloat16)
    input_grad = lax.dot_general(
        aggregated, weight, (((1,), (1,)), ((), ())), preferred_element_type=jnp.float32
    ).astype(jnp.bfloat16)
    weight_term = lax.dot_general(
        features, aggregated, (((0,), (0,)), ((), ())), preferred_element_type=jnp.float32
    )
    node_total = slab_rows * blocks
    weight_grad = all_reduce_by_exchange(weight_term) * (1.0 / math.sqrt(node_total))
    return (input_grad, weight_grad)


def solution(mesh):
    return jax.shard_map(
        per_device,
        mesh=mesh,
        in_specs=(
            P(("blk", "rep"), None),
            P("blk", None),
            P(),
            P("blk", "rep", None, None, None),
            P("blk", "rep", None, None),
            P("blk", "rep"),
            P("blk"),
        ),
        out_specs=(P(("blk", "rep"), None), P()),
        check_vma=False,
    )
```

```python
import functools
import math

import jax
import jax.numpy as jnp
from jax import lax
from jax.experimental import pallas as pl
from jax.experimental.pallas import tpu as pltpu
from jax.sharding import PartitionSpec as P

CHUNKS = 4
MESH_ID = pl.DeviceIdType.MESH


def gather_kernel(steps, blocks, slab_ref, out_ref, send_sem, recv_sem):
    me = lax.axis_index("blk")
    rep = lax.axis_index("rep")
    rows = slab_ref.shape[0] // CHUNKS
    centre = steps // 2
    reach = steps * rep + centre
    far_to = lax.rem(me - reach + blocks * steps, blocks)
    far_from = lax.rem(me + reach, blocks)
    left = lax.rem(me + blocks - 1, blocks)
    right = lax.rem(me + 1, blocks)

    barrier = pltpu.get_barrier_semaphore()
    for partner in (left, right, far_to, far_from):
        pl.semaphore_signal(barrier, inc=1, device_id=(partner, rep), device_id_type=MESH_ID)
    pl.semaphore_wait(barrier, 4)

    def part(c):
        return pl.ds(c * rows, rows)

    def copy(src_slot, dst_slot, c, target):
        src = slab_ref.at[part(c)] if src_slot is None else out_ref.at[src_slot, part(c)]
        return pltpu.make_async_remote_copy(
            src_ref=src,
            dst_ref=out_ref.at[dst_slot, part(c)],
            send_sem=send_sem.at[dst_slot, c],
            recv_sem=recv_sem.at[dst_slot, c],
            device_id=(target, rep),
            device_id_type=MESH_ID,
        )

    for c in range(CHUNKS):
        copy(None, centre, c, far_to).start()

    sent = []
    for k in range(1, centre + 1):
        for c in range(CHUNKS):
            up = centre + k
            down = centre - k
            if up < steps:
                copy(up - 1, up - 1, c, left).wait_recv()
                forward = copy(up - 1, up, c, left)
                forward.start()
                sent.append(forward)
            if down >= 0:
                if k > 1 or up >= steps:
                    copy(down + 1, down + 1, c, right).wait_recv()
                forward = copy(down + 1, down, c, right)
                forward.start()
                sent.append(forward)

    for c in range(CHUNKS):
        copy(None, steps - 1, c, left).wait_recv()
        copy(None, 0, c, right).wait_recv()
    for c in range(CHUNKS):
        copy(None, centre, c, far_to).wait_send()
    for forward in sent:
        forward.wait_send()


def gather_sources(scaled, steps, blocks):
    slab_rows, width = scaled.shape
    return pl.pallas_call(
        functools.partial(gather_kernel, steps, blocks),
        out_shape=jax.ShapeDtypeStruct((steps, slab_rows, width), scaled.dtype),
        in_specs=[pl.BlockSpec(memory_space=pl.ANY)],
        out_specs=pl.BlockSpec(memory_space=pl.ANY),
        scratch_shapes=[
            pltpu.SemaphoreType.DMA((steps, CHUNKS)),
            pltpu.SemaphoreType.DMA((steps, CHUNKS)),
        ],
        compiler_params=pltpu.CompilerParams(collective_id=0, has_side_effects=True),
    )(scaled)


def scatter_sum(flat, axis):
    size = lax.axis_size(axis)
    pieces = lax.all_to_all(flat.reshape(size, -1), axis, 0, 0, tiled=False)
    return pieces.sum(0)


def gather_all(piece, axis):
    size = lax.axis_size(axis)
    copies = jnp.broadcast_to(piece[None], (size,) + piece.shape)
    return lax.all_to_all(copies, axis, 0, 0, tiled=False).reshape(-1)


def all_reduce_by_exchange(term):
    flat = scatter_sum(scatter_sum(term.reshape(-1), "rep"), "blk")
    return gather_all(gather_all(flat, "blk"), "rep").reshape(term.shape)


def unpack_blocks(words):
    shifts = jnp.arange(8, dtype=jnp.int32)
    bit_values = jnp.bitwise_and(
        jnp.right_shift(words[..., :, None, :], shifts[:, None]), 1
    )
    return bit_values.reshape(words.shape[:-2] + (128, 128)).astype(jnp.bfloat16)


def per_device(features, out_grad, weight, block_words, block_coords, block_counts, degrees):
    slab_rows, width = out_grad.shape
    row_blocks = slab_rows // 128
    group_size = lax.axis_size("rep")
    blocks = lax.axis_size("blk")
    step_count = blocks // group_size
    rep_index = lax.axis_index("rep")
    inverse_root = lax.rsqrt(degrees.astype(jnp.float32))
    scaled = (out_grad.astype(jnp.float32) * inverse_root[:, None]).astype(jnp.bfloat16)

    sources = gather_sources(scaled, step_count, blocks).reshape(
        step_count, row_blocks, 128, width
    )
    coords = block_coords[0]
    slot_total = coords.shape[-1]
    picked = jnp.take_along_axis(sources, coords[:, 0, :, None, None], axis=1)
    transposed = unpack_blocks(block_words[0])
    contrib = jnp.einsum(
        "skvu,skuf->skvf", transposed, picked, preferred_element_type=jnp.float32
    )
    live = jnp.arange(slot_total, dtype=jnp.int32)[None, :] < block_counts[0][:, None]
    column_ids = jnp.arange(row_blocks, dtype=jnp.int32)
    placement = (
        (coords[:, 1, :, None] == column_ids[None, None, :]) & live[:, :, None]
    ).astype(jnp.float32)
    accumulated = jnp.einsum("skc,skvf->cvf", placement, contrib)

    partial_sums = accumulated.reshape(slab_rows, width)
    share_rows = slab_rows // group_size
    share_root = lax.dynamic_slice_in_dim(inverse_root, rep_index * share_rows, share_rows, 0)
    exchanged = lax.all_to_all(
        partial_sums.reshape(group_size, share_rows, width), "rep", 0, 0, tiled=False
    )
    own_sums = exchanged.sum(0)
    aggregated = (own_sums * share_root[:, None]).astype(jnp.bfloat16)
    input_grad = lax.dot_general(
        aggregated, weight, (((1,), (1,)), ((), ())), preferred_element_type=jnp.float32
    ).astype(jnp.bfloat16)
    weight_term = lax.dot_general(
        features, aggregated, (((0,), (0,)), ((), ())), preferred_element_type=jnp.float32
    )
    node_total = slab_rows * blocks
    weight_grad = all_reduce_by_exchange(weight_term) * (1.0 / math.sqrt(node_total))
    return (input_grad, weight_grad)


def solution(mesh):
    return jax.shard_map(
        per_device,
        mesh=mesh,
        in_specs=(
            P(("blk", "rep"), None),
            P("blk", None),
            P(),
            P("blk", "rep", None, None, None),
            P("blk", "rep", None, None),
            P("blk", "rep"),
            P("blk"),
        ),
        out_specs=(P(("blk", "rep"), None), P()),
        check_vma=False,
    )
```

```python
import functools
import math

import jax
import jax.numpy as jnp
from jax import lax
from jax.experimental import pallas as pl
from jax.experimental.pallas import tpu as pltpu
from jax.sharding import PartitionSpec as P

CHUNKS = 4
MESH_ID = pl.DeviceIdType.MESH


def gather_kernel(steps, blocks, slab_ref, out_ref, send_sem, recv_sem):
    me = lax.axis_index("blk")
    rep = lax.axis_index("rep")
    rows = slab_ref.shape[0] // CHUNKS
    centre = steps // 2
    reach = steps * rep + centre
    far_to = lax.rem(me - reach + blocks * steps, blocks)
    far_from = lax.rem(me + reach, blocks)
    left = lax.rem(me + blocks - 1, blocks)
    right = lax.rem(me + 1, blocks)

    barrier = pltpu.get_barrier_semaphore()
    for partner in (left, right, far_to, far_from):
        pl.semaphore_signal(barrier, inc=1, device_id=(partner, rep), device_id_type=MESH_ID)
    pl.semaphore_wait(barrier, 4)

    def part(c):
        return pl.ds(c * rows, rows)

    def copy(src_slot, dst_slot, c, target):
        src = slab_ref.at[part(c)] if src_slot is None else out_ref.at[src_slot, part(c)]
        return pltpu.make_async_remote_copy(
            src_ref=src,
            dst_ref=out_ref.at[dst_slot, part(c)],
            send_sem=send_sem.at[dst_slot, c],
            recv_sem=recv_sem.at[dst_slot, c],
            device_id=(target, rep),
            device_id_type=MESH_ID,
        )

    for c in range(CHUNKS):
        copy(None, centre, c, far_to).start()

    sent = []
    for k in range(1, centre + 1):
        for c in range(CHUNKS):
            up = centre + k
            down = centre - k
            if up < steps:
                copy(up - 1, up - 1, c, left).wait_recv()
                forward = copy(up - 1, up, c, left)
                forward.start()
                sent.append(forward)
            if down >= 0:
                if k > 1 or up >= steps:
                    copy(down + 1, down + 1, c, right).wait_recv()
                forward = copy(down + 1, down, c, right)
                forward.start()
                sent.append(forward)

    for c in range(CHUNKS):
        copy(None, steps - 1, c, left).wait_recv()
        copy(None, 0, c, right).wait_recv()
    for c in range(CHUNKS):
        copy(None, centre, c, far_to).wait_send()
    for forward in sent:
        forward.wait_send()


def gather_sources(scaled, steps, blocks):
    slab_rows, width = scaled.shape
    return pl.pallas_call(
        functools.partial(gather_kernel, steps, blocks),
        out_shape=jax.ShapeDtypeStruct((steps, slab_rows, width), scaled.dtype),
        in_specs=[pl.BlockSpec(memory_space=pl.ANY)],
        out_specs=pl.BlockSpec(memory_space=pl.ANY),
        scratch_shapes=[
            pltpu.SemaphoreType.DMA((steps, CHUNKS)),
            pltpu.SemaphoreType.DMA((steps, CHUNKS)),
        ],
        compiler_params=pltpu.CompilerParams(collective_id=0, has_side_effects=True),
    )(scaled)


def butterfly_kernel(levels, term_ref, out_ref, held, send_sem, recv_sem):
    me = lax.axis_index("blk")
    rep = lax.axis_index("rep")
    partners = [jnp.bitwise_xor(me, 1 << k) for k in range(levels)]
    barrier = pltpu.get_barrier_semaphore()
    for partner in partners:
        pl.semaphore_signal(barrier, inc=1, device_id=(partner, rep), device_id_type=MESH_ID)
    pl.semaphore_wait(barrier, levels)
    out_ref[...] = term_ref[...]
    for k, partner in enumerate(partners):
        swap = pltpu.make_async_remote_copy(
            src_ref=out_ref,
            dst_ref=held.at[k],
            send_sem=send_sem.at[k],
            recv_sem=recv_sem.at[k],
            device_id=(partner, rep),
            device_id_type=MESH_ID,
        )
        swap.start()
        swap.wait()
        out_ref[...] = out_ref[...] + held[k]


def butterfly_sum(term):
    levels = lax.axis_size("blk").bit_length() - 1
    return pl.pallas_call(
        functools.partial(butterfly_kernel, levels),
        out_shape=jax.ShapeDtypeStruct(term.shape, term.dtype),
        in_specs=[pl.BlockSpec(memory_space=pltpu.VMEM)],
        out_specs=pl.BlockSpec(memory_space=pltpu.VMEM),
        scratch_shapes=[
            pltpu.VMEM((levels,) + term.shape, term.dtype),
            pltpu.SemaphoreType.DMA((levels,)),
            pltpu.SemaphoreType.DMA((levels,)),
        ],
        compiler_params=pltpu.CompilerParams(collective_id=1, has_side_effects=True),
    )(term)


def scatter_sum(flat, axis):
    size = lax.axis_size(axis)
    pieces = lax.all_to_all(flat.reshape(size, -1), axis, 0, 0, tiled=False)
    return pieces.sum(0)


def gather_all(piece, axis):
    size = lax.axis_size(axis)
    copies = jnp.broadcast_to(piece[None], (size,) + piece.shape)
    return lax.all_to_all(copies, axis, 0, 0, tiled=False).reshape(-1)


def all_reduce_by_exchange(term):
    flat = scatter_sum(term.reshape(-1), "rep")
    width = term.shape[-1]
    summed = butterfly_sum(flat.reshape(-1, width)).reshape(-1)
    return gather_all(summed, "rep").reshape(term.shape)


def unpack_blocks(words):
    shifts = jnp.arange(8, dtype=jnp.int32)
    bit_values = jnp.bitwise_and(
        jnp.right_shift(words[..., :, None, :], shifts[:, None]), 1
    )
    return bit_values.reshape(words.shape[:-2] + (128, 128)).astype(jnp.bfloat16)


def per_device(features, out_grad, weight, block_words, block_coords, block_counts, degrees):
    slab_rows, width = out_grad.shape
    row_blocks = slab_rows // 128
    group_size = lax.axis_size("rep")
    blocks = lax.axis_size("blk")
    step_count = blocks // group_size
    rep_index = lax.axis_index("rep")
    inverse_root = lax.rsqrt(degrees.astype(jnp.float32))
    scaled = (out_grad.astype(jnp.float32) * inverse_root[:, None]).astype(jnp.bfloat16)

    sources = gather_sources(scaled, step_count, blocks).reshape(
        step_count, row_blocks, 128, width
    )
    coords = block_coords[0]
    slot_total = coords.shape[-1]
    picked = jnp.take_along_axis(sources, coords[:, 0, :, None, None], axis=1)
    transposed = unpack_blocks(block_words[0])
    contrib = jnp.einsum(
        "skvu,skuf->skvf", transposed, picked, preferred_element_type=jnp.float32
    )
    live = jnp.arange(slot_total, dtype=jnp.int32)[None, :] < block_counts[0][:, None]
    column_ids = jnp.arange(row_blocks, dtype=jnp.int32)
    placement = (
        (coords[:, 1, :, None] == column_ids[None, None, :]) & live[:, :, None]
    ).astype(jnp.float32)
    accumulated = jnp.einsum("skc,skvf->cvf", placement, contrib)

    partial_sums = accumulated.reshape(slab_rows, width)
    share_rows = slab_rows // group_size
    share_root = lax.dynamic_slice_in_dim(inverse_root, rep_index * share_rows, share_rows, 0)
    exchanged = lax.all_to_all(
        partial_sums.reshape(group_size, share_rows, width), "rep", 0, 0, tiled=False
    )
    own_sums = exchanged.sum(0)
    aggregated = (own_sums * share_root[:, None]).astype(jnp.bfloat16)
    input_grad = lax.dot_general(
        aggregated, weight, (((1,), (1,)), ((), ())), preferred_element_type=jnp.float32
    ).astype(jnp.bfloat16)
    weight_term = lax.dot_general(
        features, aggregated, (((0,), (0,)), ((), ())), preferred_element_type=jnp.float32
    )
    node_total = slab_rows * blocks
    weight_grad = all_reduce_by_exchange(weight_term) * (1.0 / math.sqrt(node_total))
    return (input_grad, weight_grad)


def solution(mesh):
    return jax.shard_map(
        per_device,
        mesh=mesh,
        in_specs=(
            P(("blk", "rep"), None),
            P("blk", None),
            P(),
            P("blk", "rep", None, None, None),
            P("blk", "rep", None, None),
            P("blk", "rep"),
            P("blk"),
        ),
        out_specs=(P(("blk", "rep"), None), P()),
        check_vma=False,
    )
```

```python
import functools
import math

import jax
import jax.numpy as jnp
from jax import lax
from jax.experimental import pallas as pl
from jax.experimental.pallas import tpu as pltpu
from jax.sharding import PartitionSpec as P

CHUNKS = 8
MESH_ID = pl.DeviceIdType.MESH


def relay_plan(steps, blocks, group):
    plans = []
    for rep in range(group):
        reach = steps * rep + steps // 2
        short = min(reach, blocks - reach)
        if 4 * short < 5 * blocks // 4:
            plans.append((CHUNKS, 0, 0))
            continue
        direct = min(CHUNKS, max(1, int(CHUNKS * (blocks - short) / blocks + 0.5)))
        sign = 1 if reach < blocks - reach else -1
        plans.append((direct, sign, (blocks - short) // 2))
    return plans


def gather_kernel(steps, blocks, plans, slab_ref, out_ref, relay_buf, send_sem, recv_sem,
                  relay_in_sem, relay_fwd_sem):
    me = lax.axis_index("blk")
    rep = lax.axis_index("rep")
    rows = slab_ref.shape[0] // CHUNKS
    centre = steps // 2
    reach = steps * rep + centre
    far_to = lax.rem(me - reach + blocks * steps, blocks)
    far_from = lax.rem(me + reach, blocks)
    left = lax.rem(me + blocks - 1, blocks)
    right = lax.rem(me + 1, blocks)

    def part(c):
        return pl.ds(c * rows, rows)

    def copy(src_slot, dst_slot, c, target):
        src = slab_ref.at[part(c)] if src_slot is None else out_ref.at[src_slot, part(c)]
        return pltpu.make_async_remote_copy(
            src_ref=src,
            dst_ref=out_ref.at[dst_slot, part(c)],
            send_sem=send_sem.at[dst_slot, c],
            recv_sem=recv_sem.at[dst_slot, c],
            device_id=(target, rep),
            device_id_type=MESH_ID,
        )

    def relay_out(c, target):
        return pltpu.make_async_remote_copy(
            src_ref=slab_ref.at[part(c)],
            dst_ref=relay_buf.at[c],
            send_sem=send_sem.at[centre, c],
            recv_sem=relay_in_sem.at[c],
            device_id=(target, rep),
            device_id_type=MESH_ID,
        )

    def relay_on(c, target):
        return pltpu.make_async_remote_copy(
            src_ref=relay_buf.at[c],
            dst_ref=out_ref.at[centre, part(c)],
            send_sem=relay_fwd_sem.at[c],
            recv_sem=recv_sem.at[centre, c],
            device_id=(target, rep),
            device_id_type=MESH_ID,
        )

    barrier = pltpu.get_barrier_semaphore()
    for partner in (left, right, far_to, far_from):
        pl.semaphore_signal(barrier, inc=1, device_id=(partner, rep), device_id_type=MESH_ID)

    for plane, (direct, sign, leg) in enumerate(plans):
        @pl.when(rep == plane)
        def _():
            if direct < CHUNKS:
                ahead = lax.rem(me + sign * leg + blocks, blocks)
                behind = lax.rem(me - sign * leg + blocks, blocks)
                for partner in (ahead, behind):
                    pl.semaphore_signal(barrier, inc=1, device_id=(partner, rep), device_id_type=MESH_ID)
                pl.semaphore_wait(barrier, 6)
                for c in range(direct):
                    copy(None, centre, c, far_to).start()
                for c in range(direct, CHUNKS):
                    relay_out(c, ahead).start()
                for c in range(direct, CHUNKS):
                    relay_out(c, ahead).wait_recv()
                    relay_on(c, ahead).start()
            else:
                pl.semaphore_wait(barrier, 4)
                for c in range(CHUNKS):
                    copy(None, centre, c, far_to).start()

    sent = []
    for k in range(1, centre + 1):
        for c in range(CHUNKS):
            up = centre + k
            down = centre - k
            if up < steps:
                copy(up - 1, up - 1, c, left).wait_recv()
                forward = copy(up - 1, up, c, left)
                forward.start()
                sent.append(forward)
            if down >= 0:
                if k > 1 or up >= steps:
                    copy(down + 1, down + 1, c, right).wait_recv()
                forward = copy(down + 1, down, c, right)
                forward.start()
                sent.append(forward)

    for c in range(CHUNKS):
        copy(None, steps - 1, c, left).wait_recv()
        copy(None, 0, c, right).wait_recv()

    for plane, (direct, sign, leg) in enumerate(plans):
        @pl.when(rep == plane)
        def _():
            ahead = lax.rem(me + sign * leg + blocks, blocks)
            for c in range(direct):
                copy(None, centre, c, far_to).wait_send()
            for c in range(direct, CHUNKS):
                relay_out(c, ahead).wait_send()
                relay_on(c, ahead).wait_send()
    for forward in sent:
        forward.wait_send()


def gather_sources(scaled, steps, blocks, group):
    slab_rows, width = scaled.shape
    plans = relay_plan(steps, blocks, group)
    return pl.pallas_call(
        functools.partial(gather_kernel, steps, blocks, plans),
        out_shape=jax.ShapeDtypeStruct((steps, slab_rows, width), scaled.dtype),
        in_specs=[pl.BlockSpec(memory_space=pl.ANY)],
        out_specs=pl.BlockSpec(memory_space=pl.ANY),
        scratch_shapes=[
            pltpu.VMEM((CHUNKS, slab_rows // CHUNKS, width), scaled.dtype),
            pltpu.SemaphoreType.DMA((steps, CHUNKS)),
            pltpu.SemaphoreType.DMA((steps, CHUNKS)),
            pltpu.SemaphoreType.DMA((CHUNKS,)),
            pltpu.SemaphoreType.DMA((CHUNKS,)),
        ],
        compiler_params=pltpu.CompilerParams(collective_id=0, has_side_effects=True),
    )(scaled)


def butterfly_kernel(levels, term_ref, out_ref, held, send_sem, recv_sem):
    me = lax.axis_index("blk")
    rep = lax.axis_index("rep")
    partners = [jnp.bitwise_xor(me, 1 << k) for k in range(levels)]
    barrier = pltpu.get_barrier_semaphore()
    for partner in partners:
        pl.semaphore_signal(barrier, inc=1, device_id=(partner, rep), device_id_type=MESH_ID)
    pl.semaphore_wait(barrier, levels)
    out_ref[...] = term_ref[...]
    for k, partner in enumerate(partners):
        swap = pltpu.make_async_remote_copy(
            src_ref=out_ref,
            dst_ref=held.at[k],
            send_sem=send_sem.at[k],
            recv_sem=recv_sem.at[k],
            device_id=(partner, rep),
            device_id_type=MESH_ID,
        )
        swap.start()
        swap.wait()
        out_ref[...] = out_ref[...] + held[k]


def butterfly_sum(term):
    levels = lax.axis_size("blk").bit_length() - 1
    return pl.pallas_call(
        functools.partial(butterfly_kernel, levels),
        out_shape=jax.ShapeDtypeStruct(term.shape, term.dtype),
        in_specs=[pl.BlockSpec(memory_space=pltpu.VMEM)],
        out_specs=pl.BlockSpec(memory_space=pltpu.VMEM),
        scratch_shapes=[
            pltpu.VMEM((levels,) + term.shape, term.dtype),
            pltpu.SemaphoreType.DMA((levels,)),
            pltpu.SemaphoreType.DMA((levels,)),
        ],
        compiler_params=pltpu.CompilerParams(collective_id=1, has_side_effects=True),
    )(term)


def scatter_sum(flat, axis):
    size = lax.axis_size(axis)
    pieces = lax.all_to_all(flat.reshape(size, -1), axis, 0, 0, tiled=False)
    return pieces.sum(0)


def gather_all(piece, axis):
    size = lax.axis_size(axis)
    copies = jnp.broadcast_to(piece[None], (size,) + piece.shape)
    return lax.all_to_all(copies, axis, 0, 0, tiled=False).reshape(-1)


def all_reduce_by_exchange(term):
    flat = scatter_sum(term.reshape(-1), "rep")
    width = term.shape[-1]
    summed = butterfly_sum(flat.reshape(-1, width)).reshape(-1)
    return gather_all(summed, "rep").reshape(term.shape)


def unpack_blocks(words):
    shifts = jnp.arange(8, dtype=jnp.int32)
    bit_values = jnp.bitwise_and(
        jnp.right_shift(words[..., :, None, :], shifts[:, None]), 1
    )
    return bit_values.reshape(words.shape[:-2] + (128, 128)).astype(jnp.bfloat16)


def per_device(features, out_grad, weight, block_words, block_coords, block_counts, degrees):
    slab_rows, width = out_grad.shape
    row_blocks = slab_rows // 128
    group_size = lax.axis_size("rep")
    blocks = lax.axis_size("blk")
    step_count = blocks // group_size
    rep_index = lax.axis_index("rep")
    inverse_root = lax.rsqrt(degrees.astype(jnp.float32))
    scaled = (out_grad.astype(jnp.float32) * inverse_root[:, None]).astype(jnp.bfloat16)

    sources = gather_sources(scaled, step_count, blocks, group_size).reshape(
        step_count, row_blocks, 128, width
    )
    coords = block_coords[0]
    slot_total = coords.shape[-1]
    picked = jnp.take_along_axis(sources, coords[:, 0, :, None, None], axis=1)
    transposed = unpack_blocks(block_words[0])
    contrib = jnp.einsum(
        "skvu,skuf->skvf", transposed, picked, preferred_element_type=jnp.float32
    )
    live = jnp.arange(slot_total, dtype=jnp.int32)[None, :] < block_counts[0][:, None]
    column_ids = jnp.arange(row_blocks, dtype=jnp.int32)
    placement = (
        (coords[:, 1, :, None] == column_ids[None, None, :]) & live[:, :, None]
    ).astype(jnp.float32)
    accumulated = jnp.einsum("skc,skvf->cvf", placement, contrib)

    partial_sums = accumulated.reshape(slab_rows, width)
    share_rows = slab_rows // group_size
    share_root = lax.dynamic_slice_in_dim(inverse_root, rep_index * share_rows, share_rows, 0)
    exchanged = lax.all_to_all(
        partial_sums.reshape(group_size, share_rows, width), "rep", 0, 0, tiled=False
    )
    own_sums = exchanged.sum(0)
    aggregated = (own_sums * share_root[:, None]).astype(jnp.bfloat16)
    input_grad = lax.dot_general(
        aggregated, weight, (((1,), (1,)), ((), ())), preferred_element_type=jnp.float32
    ).astype(jnp.bfloat16)
    weight_term = lax.dot_general(
        features, aggregated, (((0,), (0,)), ((), ())), preferred_element_type=jnp.float32
    )
    node_total = slab_rows * blocks
    weight_grad = all_reduce_by_exchange(weight_term) * (1.0 / math.sqrt(node_total))
    return (input_grad, weight_grad)


def solution(mesh):
    return jax.shard_map(
        per_device,
        mesh=mesh,
        in_specs=(
            P(("blk", "rep"), None),
            P("blk", None),
            P(),
            P("blk", "rep", None, None, None),
            P("blk", "rep", None, None),
            P("blk", "rep"),
            P("blk"),
        ),
        out_specs=(P(("blk", "rep"), None), P()),
        check_vma=False,
    )
```

```python
import functools
import math

import jax
import jax.numpy as jnp
from jax import lax
from jax.experimental import pallas as pl
from jax.experimental.pallas import tpu as pltpu
from jax.sharding import PartitionSpec as P

CHUNKS = 8
MESH_ID = pl.DeviceIdType.MESH


def relay_plan(steps, blocks, group):
    plans = []
    for rep in range(group):
        reach = steps * rep + steps // 2
        short = min(reach, blocks - reach)
        if 4 * short < 5 * blocks // 4:
            plans.append((CHUNKS, 0, 0))
            continue
        direct = min(CHUNKS, max(1, int(CHUNKS * (blocks - short) / blocks + 0.5)))
        sign = 1 if reach < blocks - reach else -1
        plans.append((direct, sign, (blocks - short) // 2))
    return plans


def gather_kernel(steps, blocks, plans, slab_ref, out_ref, relay_buf, send_sem, recv_sem,
                  relay_in_sem, relay_fwd_sem):
    me = lax.axis_index("blk")
    rep = lax.axis_index("rep")
    rows = slab_ref.shape[0] // CHUNKS
    centre = steps // 2
    reach = steps * rep + centre
    far_to = lax.rem(me - reach + blocks * steps, blocks)
    far_from = lax.rem(me + reach, blocks)
    left = lax.rem(me + blocks - 1, blocks)
    right = lax.rem(me + 1, blocks)

    def part(c):
        return pl.ds(c * rows, rows)

    def copy(src_slot, dst_slot, c, target):
        src = slab_ref.at[part(c)] if src_slot is None else out_ref.at[src_slot, part(c)]
        return pltpu.make_async_remote_copy(
            src_ref=src,
            dst_ref=out_ref.at[dst_slot, part(c)],
            send_sem=send_sem.at[dst_slot, c],
            recv_sem=recv_sem.at[dst_slot, c],
            device_id=(target, rep),
            device_id_type=MESH_ID,
        )

    def relay_out(c, target):
        return pltpu.make_async_remote_copy(
            src_ref=slab_ref.at[part(c)],
            dst_ref=relay_buf.at[c],
            send_sem=send_sem.at[centre, c],
            recv_sem=relay_in_sem.at[c],
            device_id=(target, rep),
            device_id_type=MESH_ID,
        )

    def relay_on(c, target):
        return pltpu.make_async_remote_copy(
            src_ref=relay_buf.at[c],
            dst_ref=out_ref.at[centre, part(c)],
            send_sem=relay_fwd_sem.at[c],
            recv_sem=recv_sem.at[centre, c],
            device_id=(target, rep),
            device_id_type=MESH_ID,
        )

    barrier = pltpu.get_barrier_semaphore()
    for partner in (left, right, far_to, far_from):
        pl.semaphore_signal(barrier, inc=1, device_id=(partner, rep), device_id_type=MESH_ID)

    for plane, (direct, sign, leg) in enumerate(plans):
        @pl.when(rep == plane)
        def _():
            if direct < CHUNKS:
                ahead = lax.rem(me + sign * leg + blocks, blocks)
                behind = lax.rem(me - sign * leg + blocks, blocks)
                for partner in (ahead, behind):
                    pl.semaphore_signal(barrier, inc=1, device_id=(partner, rep), device_id_type=MESH_ID)
                pl.semaphore_wait(barrier, 6)
                for c in range(direct):
                    copy(None, centre, c, far_to).start()
                for c in range(direct, CHUNKS):
                    relay_out(c, ahead).start()
                for c in range(direct, CHUNKS):
                    relay_out(c, ahead).wait_recv()
                    relay_on(c, ahead).start()
            else:
                pl.semaphore_wait(barrier, 4)
                for c in range(CHUNKS):
                    copy(None, centre, c, far_to).start()

    sent = []
    for k in range(1, centre + 1):
        for c in range(CHUNKS):
            up = centre + k
            down = centre - k
            if up < steps:
                copy(up - 1, up - 1, c, left).wait_recv()
                forward = copy(up - 1, up, c, left)
                forward.start()
                sent.append(forward)
            if down >= 0:
                if k > 1 or up >= steps:
                    copy(down + 1, down + 1, c, right).wait_recv()
                forward = copy(down + 1, down, c, right)
                forward.start()
                sent.append(forward)

    for c in range(CHUNKS):
        copy(None, steps - 1, c, left).wait_recv()
        copy(None, 0, c, right).wait_recv()

    for plane, (direct, sign, leg) in enumerate(plans):
        @pl.when(rep == plane)
        def _():
            ahead = lax.rem(me + sign * leg + blocks, blocks)
            for c in range(direct):
                copy(None, centre, c, far_to).wait_send()
            for c in range(direct, CHUNKS):
                relay_out(c, ahead).wait_send()
                relay_on(c, ahead).wait_send()
    for forward in sent:
        forward.wait_send()


def gather_sources(scaled, steps, blocks, group):
    slab_rows, width = scaled.shape
    plans = relay_plan(steps, blocks, group)
    return pl.pallas_call(
        functools.partial(gather_kernel, steps, blocks, plans),
        out_shape=jax.ShapeDtypeStruct((steps, slab_rows, width), scaled.dtype),
        in_specs=[pl.BlockSpec(memory_space=pl.ANY)],
        out_specs=pl.BlockSpec(memory_space=pl.ANY),
        scratch_shapes=[
            pltpu.VMEM((CHUNKS, slab_rows // CHUNKS, width), scaled.dtype),
            pltpu.SemaphoreType.DMA((steps, CHUNKS)),
            pltpu.SemaphoreType.DMA((steps, CHUNKS)),
            pltpu.SemaphoreType.DMA((CHUNKS,)),
            pltpu.SemaphoreType.DMA((CHUNKS,)),
        ],
        compiler_params=pltpu.CompilerParams(collective_id=0, has_side_effects=True),
    )(scaled)


def reduce_kernel(group, digits, term_ref, out_ref, inbox, spread, gathered, sems):
    me = lax.axis_index("blk")
    rep = lax.axis_index("rep")
    piece = term_ref.shape[0] // group
    rep_partners = [lax.rem(rep + j, group) for j in range(1, group)]
    barrier = pltpu.get_barrier_semaphore()
    for partner in rep_partners:
        pl.semaphore_signal(barrier, inc=1, device_id=(me, partner), device_id_type=MESH_ID)
    blk_count = 0
    for shift, width in digits:
        for d in range(1, 1 << width):
            pl.semaphore_signal(
                barrier, inc=1, device_id=(jnp.bitwise_xor(me, d << shift), rep), device_id_type=MESH_ID
            )
            blk_count += 1
    pl.semaphore_wait(barrier, group - 1 + blk_count)

    def send(src, dst, sem_row, slot, device):
        return pltpu.make_async_remote_copy(
            src_ref=src,
            dst_ref=dst,
            send_sem=sems.at[0, sem_row, slot],
            recv_sem=sems.at[1, sem_row, slot],
            device_id=device,
            device_id_type=MESH_ID,
        )

    scatter = []
    for j, partner in enumerate(rep_partners, start=1):
        rows = pl.ds(pl.multiple_of(partner * piece, 8), piece)
        scatter.append(send(term_ref.at[rows], inbox.at[0, j], 0, j, (me, partner)))
    for c in scatter:
        c.start()
    for c in scatter:
        c.wait()
    own = pl.ds(pl.multiple_of(rep * piece, 8), piece)
    total = term_ref[own]
    for j in range(1, group):
        total = total + inbox[0, j]
    spread[0, 0] = total

    for level, (shift, width) in enumerate(digits):
        members = 1 << width
        mine = jnp.bitwise_and(jnp.right_shift(me, shift), members - 1)
        swaps = [
            send(spread.at[level, 0], spread.at[level + 1, d], level + 1, d,
                 (jnp.bitwise_xor(me, d << shift), rep))
            for d in range(1, members)
        ]
        for c in swaps:
            c.start()
        for c in swaps:
            c.wait()
        spread[level + 1, 0] = spread[level, 0]
        total = spread[level + 1, jnp.bitwise_xor(mine, 0)]
        for i in range(1, members):
            total = total + spread[level + 1, jnp.bitwise_xor(mine, i)]
        spread[level + 1, 0] = total

    last = len(digits)
    gathered[rep] = spread[last, 0]
    spreads = [
        send(spread.at[last, 0], gathered.at[rep], last + 1, j, (me, partner))
        for j, partner in enumerate(rep_partners, start=1)
    ]
    for c in spreads:
        c.start()
    for c in spreads:
        c.wait()
    for r in range(group):
        out_ref[pl.ds(r * piece, piece)] = gathered[r]


def all_reduce_by_kernel(term):
    group = lax.axis_size("rep")
    bits = lax.axis_size("blk").bit_length() - 1
    digits = [(shift, min(3, bits - shift)) for shift in range(0, bits, 3)]
    piece = term.shape[0] // group
    return pl.pallas_call(
        functools.partial(reduce_kernel, group, digits),
        out_shape=jax.ShapeDtypeStruct(term.shape, term.dtype),
        in_specs=[pl.BlockSpec(memory_space=pltpu.VMEM)],
        out_specs=pl.BlockSpec(memory_space=pltpu.VMEM),
        scratch_shapes=[
            pltpu.VMEM((1, group, piece, term.shape[1]), term.dtype),
            pltpu.VMEM((len(digits) + 1, 8, piece, term.shape[1]), term.dtype),
            pltpu.VMEM((group, piece, term.shape[1]), term.dtype),
            pltpu.SemaphoreType.DMA((2, len(digits) + 2, 8)),
        ],
        compiler_params=pltpu.CompilerParams(collective_id=1, has_side_effects=True),
    )(term)


def unpack_blocks(words):
    shifts = jnp.arange(8, dtype=jnp.int32)
    bit_values = jnp.bitwise_and(
        jnp.right_shift(words[..., :, None, :], shifts[:, None]), 1
    )
    return bit_values.reshape(words.shape[:-2] + (128, 128)).astype(jnp.bfloat16)


def per_device(features, out_grad, weight, block_words, block_coords, block_counts, degrees):
    slab_rows, width = out_grad.shape
    row_blocks = slab_rows // 128
    group_size = lax.axis_size("rep")
    blocks = lax.axis_size("blk")
    step_count = blocks // group_size
    rep_index = lax.axis_index("rep")
    inverse_root = lax.rsqrt(degrees.astype(jnp.float32))
    scaled = (out_grad.astype(jnp.float32) * inverse_root[:, None]).astype(jnp.bfloat16)

    sources = gather_sources(scaled, step_count, blocks, group_size).reshape(
        step_count, row_blocks, 128, width
    )
    coords = block_coords[0]
    slot_total = coords.shape[-1]
    picked = jnp.take_along_axis(sources, coords[:, 0, :, None, None], axis=1)
    transposed = unpack_blocks(block_words[0])
    contrib = jnp.einsum(
        "skvu,skuf->skvf", transposed, picked, preferred_element_type=jnp.float32
    )
    live = jnp.arange(slot_total, dtype=jnp.int32)[None, :] < block_counts[0][:, None]
    column_ids = jnp.arange(row_blocks, dtype=jnp.int32)
    placement = (
        (coords[:, 1, :, None] == column_ids[None, None, :]) & live[:, :, None]
    ).astype(jnp.float32)
    accumulated = jnp.einsum("skc,skvf->cvf", placement, contrib)

    partial_sums = accumulated.reshape(slab_rows, width)
    share_rows = slab_rows // group_size
    share_root = lax.dynamic_slice_in_dim(inverse_root, rep_index * share_rows, share_rows, 0)
    exchanged = lax.all_to_all(
        partial_sums.reshape(group_size, share_rows, width), "rep", 0, 0, tiled=False
    )
    own_sums = exchanged.sum(0)
    aggregated = (own_sums * share_root[:, None]).astype(jnp.bfloat16)
    input_grad = lax.dot_general(
        aggregated, weight, (((1,), (1,)), ((), ())), preferred_element_type=jnp.float32
    ).astype(jnp.bfloat16)
    weight_term = lax.dot_general(
        features, aggregated, (((0,), (0,)), ((), ())), preferred_element_type=jnp.float32
    )
    node_total = slab_rows * blocks
    weight_grad = all_reduce_by_kernel(weight_term) * (1.0 / math.sqrt(node_total))
    return (input_grad, weight_grad)


def solution(mesh):
    return jax.shard_map(
        per_device,
        mesh=mesh,
        in_specs=(
            P(("blk", "rep"), None),
            P("blk", None),
            P(),
            P("blk", "rep", None, None, None),
            P("blk", "rep", None, None),
            P("blk", "rep"),
            P("blk"),
        ),
        out_specs=(P(("blk", "rep"), None), P()),
        check_vma=False,
    )
```

```python
import functools
import math

import jax
import jax.numpy as jnp
from jax import lax
from jax.experimental import pallas as pl
from jax.experimental.pallas import tpu as pltpu
from jax.sharding import PartitionSpec as P

CHUNKS = 8
MESH_ID = pl.DeviceIdType.MESH


def relay_plan(steps, blocks, group):
    plans = []
    for rep in range(group):
        reach = steps * rep + steps // 2
        short = min(reach, blocks - reach)
        if 4 * short < 5 * blocks // 4:
            plans.append((CHUNKS, 0, 0))
            continue
        direct = min(CHUNKS, max(1, int(CHUNKS * (blocks - short) / blocks + 0.5)))
        sign = 1 if reach < blocks - reach else -1
        plans.append((direct, sign, (blocks - short) // 2))
    return plans


def gather_kernel(steps, blocks, plans, slab_ref, out_ref, relay_buf, send_sem, recv_sem,
                  relay_in_sem, relay_fwd_sem):
    me = lax.axis_index("blk")
    rep = lax.axis_index("rep")
    rows = slab_ref.shape[0] // CHUNKS
    centre = steps // 2
    reach = steps * rep + centre
    far_to = lax.rem(me - reach + blocks * steps, blocks)
    far_from = lax.rem(me + reach, blocks)
    left = lax.rem(me + blocks - 1, blocks)
    right = lax.rem(me + 1, blocks)

    def part(c):
        return pl.ds(c * rows, rows)

    def copy(src_slot, dst_slot, c, target):
        src = slab_ref.at[part(c)] if src_slot is None else out_ref.at[src_slot, part(c)]
        return pltpu.make_async_remote_copy(
            src_ref=src,
            dst_ref=out_ref.at[dst_slot, part(c)],
            send_sem=send_sem.at[dst_slot, c],
            recv_sem=recv_sem.at[dst_slot, c],
            device_id=(target, rep),
            device_id_type=MESH_ID,
        )

    def relay_out(c, target):
        return pltpu.make_async_remote_copy(
            src_ref=slab_ref.at[part(c)],
            dst_ref=relay_buf.at[c],
            send_sem=send_sem.at[centre, c],
            recv_sem=relay_in_sem.at[c],
            device_id=(target, rep),
            device_id_type=MESH_ID,
        )

    def relay_on(c, target):
        return pltpu.make_async_remote_copy(
            src_ref=relay_buf.at[c],
            dst_ref=out_ref.at[centre, part(c)],
            send_sem=relay_fwd_sem.at[c],
            recv_sem=recv_sem.at[centre, c],
            device_id=(target, rep),
            device_id_type=MESH_ID,
        )

    barrier = pltpu.get_barrier_semaphore()
    for partner in (left, right, far_to, far_from):
        pl.semaphore_signal(barrier, inc=1, device_id=(partner, rep), device_id_type=MESH_ID)

    for plane, (direct, sign, leg) in enumerate(plans):
        @pl.when(rep == plane)
        def _():
            if direct < CHUNKS:
                ahead = lax.rem(me + sign * leg + blocks, blocks)
                behind = lax.rem(me - sign * leg + blocks, blocks)
                for partner in (ahead, behind):
                    pl.semaphore_signal(barrier, inc=1, device_id=(partner, rep), device_id_type=MESH_ID)
                pl.semaphore_wait(barrier, 6)
                for c in range(direct):
                    copy(None, centre, c, far_to).start()
                for c in range(direct, CHUNKS):
                    relay_out(c, ahead).start()
                for c in range(direct, CHUNKS):
                    relay_out(c, ahead).wait_recv()
                    relay_on(c, ahead).start()
            else:
                pl.semaphore_wait(barrier, 4)
                for c in range(CHUNKS):
                    copy(None, centre, c, far_to).start()

    sent = []
    for k in range(1, centre + 1):
        for c in range(CHUNKS):
            up = centre + k
            down = centre - k
            if up < steps:
                copy(up - 1, up - 1, c, left).wait_recv()
                forward = copy(up - 1, up, c, left)
                forward.start()
                sent.append(forward)
            if down >= 0:
                if k > 1 or up >= steps:
                    copy(down + 1, down + 1, c, right).wait_recv()
                forward = copy(down + 1, down, c, right)
                forward.start()
                sent.append(forward)

    for c in range(CHUNKS):
        copy(None, steps - 1, c, left).wait_recv()
        copy(None, 0, c, right).wait_recv()

    for plane, (direct, sign, leg) in enumerate(plans):
        @pl.when(rep == plane)
        def _():
            ahead = lax.rem(me + sign * leg + blocks, blocks)
            for c in range(direct):
                copy(None, centre, c, far_to).wait_send()
            for c in range(direct, CHUNKS):
                relay_out(c, ahead).wait_send()
                relay_on(c, ahead).wait_send()
    for forward in sent:
        forward.wait_send()


def gather_sources(scaled, steps, blocks, group):
    slab_rows, width = scaled.shape
    plans = relay_plan(steps, blocks, group)
    return pl.pallas_call(
        functools.partial(gather_kernel, steps, blocks, plans),
        out_shape=jax.ShapeDtypeStruct((steps, slab_rows, width), scaled.dtype),
        in_specs=[pl.BlockSpec(memory_space=pl.ANY)],
        out_specs=pl.BlockSpec(memory_space=pl.ANY),
        scratch_shapes=[
            pltpu.VMEM((CHUNKS, slab_rows // CHUNKS, width), scaled.dtype),
            pltpu.SemaphoreType.DMA((steps, CHUNKS)),
            pltpu.SemaphoreType.DMA((steps, CHUNKS)),
            pltpu.SemaphoreType.DMA((CHUNKS,)),
            pltpu.SemaphoreType.DMA((CHUNKS,)),
        ],
        compiler_params=pltpu.CompilerParams(collective_id=0, has_side_effects=True),
    )(scaled)


def finish_kernel(group, digits, partial_ref, root_ref, feat_t_ref, weight_t_ref, grad_ref, out_ref,
                  sums_in, inbox, spread, gathered, sems):
    me = lax.axis_index("blk")
    rep = lax.axis_index("rep")
    share = grad_ref.shape[0]
    piece = out_ref.shape[0] // group
    rep_partners = [lax.rem(rep + j, group) for j in range(1, group)]
    barrier = pltpu.get_barrier_semaphore()
    for partner in rep_partners:
        pl.semaphore_signal(barrier, inc=1, device_id=(me, partner), device_id_type=MESH_ID)
    blk_count = 0
    for shift, width in digits:
        for d in range(1, 1 << width):
            pl.semaphore_signal(
                barrier, inc=1, device_id=(jnp.bitwise_xor(me, d << shift), rep), device_id_type=MESH_ID
            )
            blk_count += 1
    pl.semaphore_wait(barrier, group - 1 + blk_count)

    def send(src, dst, sem_row, slot, device):
        return pltpu.make_async_remote_copy(
            src_ref=src,
            dst_ref=dst,
            send_sem=sems.at[0, sem_row, slot],
            recv_sem=sems.at[1, sem_row, slot],
            device_id=device,
            device_id_type=MESH_ID,
        )

    shares = []
    for j, partner in enumerate(rep_partners, start=1):
        rows = pl.ds(pl.multiple_of(partner * share, 8), share)
        shares.append(send(partial_ref.at[rows], sums_in.at[j], 0, j, (me, partner)))
    for c in shares:
        c.start()
    for c in shares:
        c.wait()
    own_rows = pl.ds(pl.multiple_of(rep * share, 8), share)
    summed = partial_ref[own_rows]
    for j in range(1, group):
        summed = summed + sums_in[j]
    aggregated = (summed * root_ref[...]).astype(jnp.bfloat16)
    grad_ref[...] = jnp.dot(
        aggregated, weight_t_ref[...], preferred_element_type=jnp.float32
    ).astype(grad_ref.dtype)
    term = jnp.dot(feat_t_ref[...], aggregated, preferred_element_type=jnp.float32)
    spread[0, 0] = term

    scatter = []
    for j, partner in enumerate(rep_partners, start=1):
        rows = pl.ds(pl.multiple_of(partner * piece, 8), piece)
        scatter.append(send(spread.at[0, 0, rows], inbox.at[j], 1, j, (me, partner)))
    for c in scatter:
        c.start()
    for c in scatter:
        c.wait()
    own = pl.ds(pl.multiple_of(rep * piece, 8), piece)
    total = spread[0, 0, own]
    for j in range(1, group):
        total = total + inbox[j]
    spread[1, 0, pl.ds(0, piece)] = total

    for level, (shift, width) in enumerate(digits, start=1):
        members = 1 << width
        mine = jnp.bitwise_and(jnp.right_shift(me, shift), members - 1)
        swaps = [
            send(spread.at[level, 0, pl.ds(0, piece)], spread.at[level + 1, d, pl.ds(0, piece)],
                 level + 1, d, (jnp.bitwise_xor(me, d << shift), rep))
            for d in range(1, members)
        ]
        for c in swaps:
            c.start()
        for c in swaps:
            c.wait()
        spread[level + 1, 0, pl.ds(0, piece)] = spread[level, 0, pl.ds(0, piece)]
        total = spread[level + 1, mine, pl.ds(0, piece)]
        for i in range(1, members):
            total = total + spread[level + 1, jnp.bitwise_xor(mine, i), pl.ds(0, piece)]
        spread[level + 1, 0, pl.ds(0, piece)] = total

    last = len(digits) + 1
    gathered[rep] = spread[last, 0, pl.ds(0, piece)]
    spreads = [
        send(spread.at[last, 0, pl.ds(0, piece)], gathered.at[rep], last + 1, j, (me, partner))
        for j, partner in enumerate(rep_partners, start=1)
    ]
    for c in spreads:
        c.start()
    for c in spreads:
        c.wait()
    for r in range(group):
        out_ref[pl.ds(r * piece, piece)] = gathered[r]


def finish(partial_sums, share_root, features, weight):
    group = lax.axis_size("rep")
    bits = lax.axis_size("blk").bit_length() - 1
    digits = [(shift, min(3, bits - shift)) for shift in range(0, bits, 3)]
    slab_rows, width = partial_sums.shape
    share = slab_rows // group
    fan = weight.shape[1]
    piece = fan // group
    vmem = pl.BlockSpec(memory_space=pltpu.VMEM)
    return pl.pallas_call(
        functools.partial(finish_kernel, group, digits),
        out_shape=(
            jax.ShapeDtypeStruct((share, weight.shape[0]), jnp.bfloat16),
            jax.ShapeDtypeStruct((fan, width), jnp.float32),
        ),
        in_specs=[vmem] * 4,
        out_specs=(vmem, vmem),
        scratch_shapes=[
            pltpu.VMEM((group, share, width), jnp.float32),
            pltpu.VMEM((group, piece, width), jnp.float32),
            pltpu.VMEM((len(digits) + 2, 8, fan, width), jnp.float32),
            pltpu.VMEM((group, piece, width), jnp.float32),
            pltpu.SemaphoreType.DMA((2, len(digits) + 3, 8)),
        ],
        compiler_params=pltpu.CompilerParams(collective_id=1, has_side_effects=True),
    )(partial_sums, share_root[:, None], features.T, weight.T)


def unpack_blocks(words):
    shifts = jnp.arange(8, dtype=jnp.int32)
    bit_values = jnp.bitwise_and(
        jnp.right_shift(words[..., :, None, :], shifts[:, None]), 1
    )
    return bit_values.reshape(words.shape[:-2] + (128, 128)).astype(jnp.bfloat16)


def per_device(features, out_grad, weight, block_words, block_coords, block_counts, degrees):
    slab_rows, width = out_grad.shape
    row_blocks = slab_rows // 128
    group_size = lax.axis_size("rep")
    blocks = lax.axis_size("blk")
    step_count = blocks // group_size
    rep_index = lax.axis_index("rep")
    inverse_root = lax.rsqrt(degrees.astype(jnp.float32))
    scaled = (out_grad.astype(jnp.float32) * inverse_root[:, None]).astype(jnp.bfloat16)

    sources = gather_sources(scaled, step_count, blocks, group_size).reshape(
        step_count, row_blocks, 128, width
    )
    coords = block_coords[0]
    slot_total = coords.shape[-1]
    picked = jnp.take_along_axis(sources, coords[:, 0, :, None, None], axis=1)
    transposed = unpack_blocks(block_words[0])
    contrib = jnp.einsum(
        "skvu,skuf->skvf", transposed, picked, preferred_element_type=jnp.float32
    )
    live = jnp.arange(slot_total, dtype=jnp.int32)[None, :] < block_counts[0][:, None]
    column_ids = jnp.arange(row_blocks, dtype=jnp.int32)
    placement = (
        (coords[:, 1, :, None] == column_ids[None, None, :]) & live[:, :, None]
    ).astype(jnp.float32)
    accumulated = jnp.einsum("skc,skvf->cvf", placement, contrib)

    partial_sums = accumulated.reshape(slab_rows, width)
    share_rows = slab_rows // group_size
    share_root = lax.dynamic_slice_in_dim(inverse_root, rep_index * share_rows, share_rows, 0)
    input_grad, weight_sum = finish(partial_sums, share_root, features, weight)
    node_total = slab_rows * blocks
    weight_grad = weight_sum * (1.0 / math.sqrt(node_total))
    return (input_grad, weight_grad)


def solution(mesh):
    return jax.shard_map(
        per_device,
        mesh=mesh,
        in_specs=(
            P(("blk", "rep"), None),
            P("blk", None),
            P(),
            P("blk", "rep", None, None, None),
            P("blk", "rep", None, None),
            P("blk", "rep"),
            P("blk"),
        ),
        out_specs=(P(("blk", "rep"), None), P()),
        check_vma=False,
    )
```

```python
import functools
import math

import jax
import jax.numpy as jnp
from jax import lax
from jax.experimental import pallas as pl
from jax.experimental.pallas import tpu as pltpu
from jax.sharding import PartitionSpec as P

CHUNKS = 16
MESH_ID = pl.DeviceIdType.MESH


def relay_plan(steps, blocks, group):
    plans = []
    for rep in range(group):
        reach = steps * rep + steps // 2
        short = min(reach, blocks - reach)
        if 16 * short < 3 * blocks:
            plans.append((CHUNKS, 0, 0))
            continue
        direct = min(CHUNKS, max(1, int(CHUNKS * (blocks - short) / blocks + 0.5)))
        sign = 1 if reach < blocks - reach else -1
        plans.append((direct, sign, (blocks - short) // 2))
    return plans


def gather_kernel(steps, blocks, plans, slab_ref, out_ref, relay_buf, send_sem, recv_sem,
                  relay_in_sem, relay_fwd_sem):
    me = lax.axis_index("blk")
    rep = lax.axis_index("rep")
    rows = slab_ref.shape[0] // CHUNKS
    centre = steps // 2
    reach = steps * rep + centre
    far_to = lax.rem(me - reach + blocks * steps, blocks)
    far_from = lax.rem(me + reach, blocks)
    left = lax.rem(me + blocks - 1, blocks)
    right = lax.rem(me + 1, blocks)

    def part(c):
        return pl.ds(c * rows, rows)

    def copy(src_slot, dst_slot, c, target):
        src = slab_ref.at[part(c)] if src_slot is None else out_ref.at[src_slot, part(c)]
        return pltpu.make_async_remote_copy(
            src_ref=src,
            dst_ref=out_ref.at[dst_slot, part(c)],
            send_sem=send_sem.at[dst_slot, c],
            recv_sem=recv_sem.at[dst_slot, c],
            device_id=(target, rep),
            device_id_type=MESH_ID,
        )

    def relay_out(c, target):
        return pltpu.make_async_remote_copy(
            src_ref=slab_ref.at[part(c)],
            dst_ref=relay_buf.at[c],
            send_sem=send_sem.at[centre, c],
            recv_sem=relay_in_sem.at[c],
            device_id=(target, rep),
            device_id_type=MESH_ID,
        )

    def relay_on(c, target):
        return pltpu.make_async_remote_copy(
            src_ref=relay_buf.at[c],
            dst_ref=out_ref.at[centre, part(c)],
            send_sem=relay_fwd_sem.at[c],
            recv_sem=recv_sem.at[centre, c],
            device_id=(target, rep),
            device_id_type=MESH_ID,
        )

    barrier = pltpu.get_barrier_semaphore()
    for partner in (left, right, far_to, far_from):
        pl.semaphore_signal(barrier, inc=1, device_id=(partner, rep), device_id_type=MESH_ID)

    for plane, (direct, sign, leg) in enumerate(plans):
        @pl.when(rep == plane)
        def _():
            if direct < CHUNKS:
                ahead = lax.rem(me + sign * leg + blocks, blocks)
                behind = lax.rem(me - sign * leg + blocks, blocks)
                for partner in (ahead, behind):
                    pl.semaphore_signal(barrier, inc=1, device_id=(partner, rep), device_id_type=MESH_ID)
                pl.semaphore_wait(barrier, 6)
                for c in range(direct):
                    copy(None, centre, c, far_to).start()
                for c in range(direct, CHUNKS):
                    relay_out(c, ahead).start()
                for c in range(direct, CHUNKS):
                    relay_out(c, ahead).wait_recv()
                    relay_on(c, ahead).start()
            else:
                pl.semaphore_wait(barrier, 4)
                for c in range(CHUNKS):
                    copy(None, centre, c, far_to).start()

    sent = []
    for k in range(1, centre + 1):
        for c in range(CHUNKS):
            up = centre + k
            down = centre - k
            if up < steps:
                copy(up - 1, up - 1, c, left).wait_recv()
                forward = copy(up - 1, up, c, left)
                forward.start()
                sent.append(forward)
            if down >= 0:
                if k > 1 or up >= steps:
                    copy(down + 1, down + 1, c, right).wait_recv()
                forward = copy(down + 1, down, c, right)
                forward.start()
                sent.append(forward)

    for c in range(CHUNKS):
        copy(None, steps - 1, c, left).wait_recv()
        copy(None, 0, c, right).wait_recv()

    for plane, (direct, sign, leg) in enumerate(plans):
        @pl.when(rep == plane)
        def _():
            ahead = lax.rem(me + sign * leg + blocks, blocks)
            for c in range(direct):
                copy(None, centre, c, far_to).wait_send()
            for c in range(direct, CHUNKS):
                relay_out(c, ahead).wait_send()
                relay_on(c, ahead).wait_send()
    for forward in sent:
        forward.wait_send()


def gather_sources(scaled, steps, blocks, group):
    slab_rows, width = scaled.shape
    plans = relay_plan(steps, blocks, group)
    return pl.pallas_call(
        functools.partial(gather_kernel, steps, blocks, plans),
        out_shape=jax.ShapeDtypeStruct((steps, slab_rows, width), scaled.dtype),
        in_specs=[pl.BlockSpec(memory_space=pl.ANY)],
        out_specs=pl.BlockSpec(memory_space=pl.ANY),
        scratch_shapes=[
            pltpu.VMEM((CHUNKS, slab_rows // CHUNKS, width), scaled.dtype),
            pltpu.SemaphoreType.DMA((steps, CHUNKS)),
            pltpu.SemaphoreType.DMA((steps, CHUNKS)),
            pltpu.SemaphoreType.DMA((CHUNKS,)),
            pltpu.SemaphoreType.DMA((CHUNKS,)),
        ],
        compiler_params=pltpu.CompilerParams(collective_id=0, has_side_effects=True),
    )(scaled)


def finish_kernel(group, digits, partial_ref, root_ref, feat_t_ref, weight_t_ref, grad_ref, out_ref,
                  sums_in, inbox, spread, gathered, sems):
    me = lax.axis_index("blk")
    rep = lax.axis_index("rep")
    share = grad_ref.shape[0]
    piece = out_ref.shape[0] // group
    rep_partners = [lax.rem(rep + j, group) for j in range(1, group)]
    barrier = pltpu.get_barrier_semaphore()
    for partner in rep_partners:
        pl.semaphore_signal(barrier, inc=1, device_id=(me, partner), device_id_type=MESH_ID)
    blk_count = 0
    for shift, width in digits:
        for d in range(1, 1 << width):
            pl.semaphore_signal(
                barrier, inc=1, device_id=(jnp.bitwise_xor(me, d << shift), rep), device_id_type=MESH_ID
            )
            blk_count += 1
    pl.semaphore_wait(barrier, group - 1 + blk_count)

    def send(src, dst, sem_row, slot, device):
        return pltpu.make_async_remote_copy(
            src_ref=src,
            dst_ref=dst,
            send_sem=sems.at[0, sem_row, slot],
            recv_sem=sems.at[1, sem_row, slot],
            device_id=device,
            device_id_type=MESH_ID,
        )

    shares = []
    for j, partner in enumerate(rep_partners, start=1):
        rows = pl.ds(pl.multiple_of(partner * share, 8), share)
        shares.append(send(partial_ref.at[rows], sums_in.at[j], 0, j, (me, partner)))
    for c in shares:
        c.start()
    for c in shares:
        c.wait()
    own_rows = pl.ds(pl.multiple_of(rep * share, 8), share)
    summed = partial_ref[own_rows].astype(jnp.float32)
    for j in range(1, group):
        summed = summed + sums_in[j].astype(jnp.float32)
    aggregated = (summed * root_ref[...]).astype(jnp.bfloat16)
    grad_ref[...] = jnp.dot(
        aggregated, weight_t_ref[...], preferred_element_type=jnp.float32
    ).astype(grad_ref.dtype)
    term = jnp.dot(feat_t_ref[...], aggregated, preferred_element_type=jnp.float32)
    spread[0, 0] = term

    scatter = []
    for j, partner in enumerate(rep_partners, start=1):
        rows = pl.ds(pl.multiple_of(partner * piece, 8), piece)
        scatter.append(send(spread.at[0, 0, rows], inbox.at[j], 1, j, (me, partner)))
    for c in scatter:
        c.start()
    for c in scatter:
        c.wait()
    own = pl.ds(pl.multiple_of(rep * piece, 8), piece)
    total = spread[0, 0, own]
    for j in range(1, group):
        total = total + inbox[j]
    spread[1, 0, pl.ds(0, piece)] = total

    for level, (shift, width) in enumerate(digits, start=1):
        members = 1 << width
        mine = jnp.bitwise_and(jnp.right_shift(me, shift), members - 1)
        swaps = [
            send(spread.at[level, 0, pl.ds(0, piece)], spread.at[level + 1, d, pl.ds(0, piece)],
                 level + 1, d, (jnp.bitwise_xor(me, d << shift), rep))
            for d in range(1, members)
        ]
        for c in swaps:
            c.start()
        for c in swaps:
            c.wait()
        spread[level + 1, 0, pl.ds(0, piece)] = spread[level, 0, pl.ds(0, piece)]
        total = spread[level + 1, mine, pl.ds(0, piece)]
        for i in range(1, members):
            total = total + spread[level + 1, jnp.bitwise_xor(mine, i), pl.ds(0, piece)]
        spread[level + 1, 0, pl.ds(0, piece)] = total

    last = len(digits) + 1
    gathered[rep] = spread[last, 0, pl.ds(0, piece)]
    spreads = [
        send(spread.at[last, 0, pl.ds(0, piece)], gathered.at[rep], last + 1, j, (me, partner))
        for j, partner in enumerate(rep_partners, start=1)
    ]
    for c in spreads:
        c.start()
    for c in spreads:
        c.wait()
    for r in range(group):
        out_ref[pl.ds(r * piece, piece)] = gathered[r]


def finish(partial_sums, share_root, features, weight):
    group = lax.axis_size("rep")
    bits = lax.axis_size("blk").bit_length() - 1
    digits = [(shift, min(3, bits - shift)) for shift in range(0, bits, 3)]
    slab_rows, width = partial_sums.shape
    share = slab_rows // group
    fan = weight.shape[1]
    piece = fan // group
    vmem = pl.BlockSpec(memory_space=pltpu.VMEM)
    return pl.pallas_call(
        functools.partial(finish_kernel, group, digits),
        out_shape=(
            jax.ShapeDtypeStruct((share, weight.shape[0]), jnp.bfloat16),
            jax.ShapeDtypeStruct((fan, width), jnp.float32),
        ),
        in_specs=[vmem] * 4,
        out_specs=(vmem, vmem),
        scratch_shapes=[
            pltpu.VMEM((group, share, width), partial_sums.dtype),
            pltpu.VMEM((group, piece, width), jnp.float32),
            pltpu.VMEM((len(digits) + 2, 8, fan, width), jnp.float32),
            pltpu.VMEM((group, piece, width), jnp.float32),
            pltpu.SemaphoreType.DMA((2, len(digits) + 3, 8)),
        ],
        compiler_params=pltpu.CompilerParams(collective_id=1, has_side_effects=True),
    )(partial_sums, share_root[:, None], features.T, weight.T)


def unpack_blocks(words):
    shifts = jnp.arange(8, dtype=jnp.int32)
    bit_values = jnp.bitwise_and(
        jnp.right_shift(words[..., :, None, :], shifts[:, None]), 1
    )
    return bit_values.reshape(words.shape[:-2] + (128, 128)).astype(jnp.bfloat16)


def per_device(features, out_grad, weight, block_words, block_coords, block_counts, degrees):
    slab_rows, width = out_grad.shape
    row_blocks = slab_rows // 128
    group_size = lax.axis_size("rep")
    blocks = lax.axis_size("blk")
    step_count = blocks // group_size
    rep_index = lax.axis_index("rep")
    inverse_root = lax.rsqrt(degrees.astype(jnp.float32))
    scaled = (out_grad.astype(jnp.float32) * inverse_root[:, None]).astype(jnp.bfloat16)

    sources = gather_sources(scaled, step_count, blocks, group_size).reshape(
        step_count, row_blocks, 128, width
    )
    coords = block_coords[0]
    slot_total = coords.shape[-1]
    picked = jnp.take_along_axis(sources, coords[:, 0, :, None, None], axis=1)
    transposed = unpack_blocks(block_words[0])
    contrib = jnp.einsum(
        "skvu,skuf->skvf", transposed, picked, preferred_element_type=jnp.float32
    )
    live = jnp.arange(slot_total, dtype=jnp.int32)[None, :] < block_counts[0][:, None]
    column_ids = jnp.arange(row_blocks, dtype=jnp.int32)
    placement = (
        (coords[:, 1, :, None] == column_ids[None, None, :]) & live[:, :, None]
    ).astype(jnp.float32)
    accumulated = jnp.einsum("skc,skvf->cvf", placement, contrib)

    partial_sums = accumulated.reshape(slab_rows, width)
    share_rows = slab_rows // group_size
    share_root = lax.dynamic_slice_in_dim(inverse_root, rep_index * share_rows, share_rows, 0)
    input_grad, weight_sum = finish(partial_sums.astype(jnp.bfloat16), share_root, features, weight)
    node_total = slab_rows * blocks
    weight_grad = weight_sum * (1.0 / math.sqrt(node_total))
    return (input_grad, weight_grad)


def solution(mesh):
    return jax.shard_map(
        per_device,
        mesh=mesh,
        in_specs=(
            P(("blk", "rep"), None),
            P("blk", None),
            P(),
            P("blk", "rep", None, None, None),
            P("blk", "rep", None, None),
            P("blk", "rep"),
            P("blk"),
        ),
        out_specs=(P(("blk", "rep"), None), P()),
        check_vma=False,
    )
```

```python
import functools
import math

import jax
import jax.numpy as jnp
from jax import lax
from jax.experimental import pallas as pl
from jax.experimental.pallas import tpu as pltpu
from jax.sharding import PartitionSpec as P

CHUNKS = 16
MESH_ID = pl.DeviceIdType.MESH


def relay_plan(steps, blocks, group):
    plans = []
    for rep in range(group):
        reach = steps * rep + steps // 2
        short = min(reach, blocks - reach)
        if 16 * short < 3 * blocks:
            plans.append((CHUNKS, 0, 0))
            continue
        direct = min(CHUNKS, max(1, int(CHUNKS * (blocks - short) / blocks + 0.5)))
        sign = 1 if reach < blocks - reach else -1
        plans.append((direct, sign, (blocks - short) // 2))
    return plans


def gather_kernel(steps, blocks, plans, group, slab_ref, feat_ref, out_ref, feats_ref, relay_buf,
                  send_sem, recv_sem, relay_in_sem, relay_fwd_sem, feat_sem):
    me = lax.axis_index("blk")
    rep = lax.axis_index("rep")
    rows = slab_ref.shape[0] // CHUNKS
    centre = steps // 2
    reach = steps * rep + centre
    far_to = lax.rem(me - reach + blocks * steps, blocks)
    far_from = lax.rem(me + reach, blocks)
    left = lax.rem(me + blocks - 1, blocks)
    right = lax.rem(me + 1, blocks)

    def part(c):
        return pl.ds(c * rows, rows)

    def copy(src_slot, dst_slot, c, target):
        src = slab_ref.at[part(c)] if src_slot is None else out_ref.at[src_slot, part(c)]
        return pltpu.make_async_remote_copy(
            src_ref=src,
            dst_ref=out_ref.at[dst_slot, part(c)],
            send_sem=send_sem.at[dst_slot, c],
            recv_sem=recv_sem.at[dst_slot, c],
            device_id=(target, rep),
            device_id_type=MESH_ID,
        )

    def relay_out(c, target):
        return pltpu.make_async_remote_copy(
            src_ref=slab_ref.at[part(c)],
            dst_ref=relay_buf.at[c],
            send_sem=send_sem.at[centre, c],
            recv_sem=relay_in_sem.at[c],
            device_id=(target, rep),
            device_id_type=MESH_ID,
        )

    def relay_on(c, target):
        return pltpu.make_async_remote_copy(
            src_ref=relay_buf.at[c],
            dst_ref=out_ref.at[centre, part(c)],
            send_sem=relay_fwd_sem.at[c],
            recv_sem=recv_sem.at[centre, c],
            device_id=(target, rep),
            device_id_type=MESH_ID,
        )

    rep_partners = [lax.rem(rep + j, group) for j in range(1, group)]

    def feat_copy(j, partner):
        return pltpu.make_async_remote_copy(
            src_ref=feat_ref,
            dst_ref=feats_ref.at[rep],
            send_sem=feat_sem.at[0, j],
            recv_sem=feat_sem.at[1, j],
            device_id=(me, partner),
            device_id_type=MESH_ID,
        )

    barrier = pltpu.get_barrier_semaphore()
    for partner in (left, right, far_to, far_from):
        pl.semaphore_signal(barrier, inc=1, device_id=(partner, rep), device_id_type=MESH_ID)
    for partner in rep_partners:
        pl.semaphore_signal(barrier, inc=1, device_id=(me, partner), device_id_type=MESH_ID)
    own_feat = pltpu.make_async_copy(feat_ref, feats_ref.at[rep], feat_sem.at[0, 0])
    own_feat.start()

    for plane, (direct, sign, leg) in enumerate(plans):
        @pl.when(rep == plane)
        def _():
            if direct < CHUNKS:
                ahead = lax.rem(me + sign * leg + blocks, blocks)
                behind = lax.rem(me - sign * leg + blocks, blocks)
                for partner in (ahead, behind):
                    pl.semaphore_signal(barrier, inc=1, device_id=(partner, rep), device_id_type=MESH_ID)
                pl.semaphore_wait(barrier, 6 + group - 1)
                for c in range(direct):
                    copy(None, centre, c, far_to).start()
                for j, partner in enumerate(rep_partners, start=1):
                    feat_copy(j, partner).start()
                for c in range(direct, CHUNKS):
                    relay_out(c, ahead).start()
                for c in range(direct, CHUNKS):
                    relay_out(c, ahead).wait_recv()
                    relay_on(c, ahead).start()
            else:
                pl.semaphore_wait(barrier, 4 + group - 1)
                for c in range(CHUNKS):
                    copy(None, centre, c, far_to).start()
                for j, partner in enumerate(rep_partners, start=1):
                    feat_copy(j, partner).start()

    sent = []
    for k in range(1, centre + 1):
        for c in range(CHUNKS):
            up = centre + k
            down = centre - k
            if up < steps:
                copy(up - 1, up - 1, c, left).wait_recv()
                forward = copy(up - 1, up, c, left)
                forward.start()
                sent.append(forward)
            if down >= 0:
                if k > 1 or up >= steps:
                    copy(down + 1, down + 1, c, right).wait_recv()
                forward = copy(down + 1, down, c, right)
                forward.start()
                sent.append(forward)

    for c in range(CHUNKS):
        copy(None, steps - 1, c, left).wait_recv()
        copy(None, 0, c, right).wait_recv()

    for plane, (direct, sign, leg) in enumerate(plans):
        @pl.when(rep == plane)
        def _():
            ahead = lax.rem(me + sign * leg + blocks, blocks)
            for c in range(direct):
                copy(None, centre, c, far_to).wait_send()
            for c in range(direct, CHUNKS):
                relay_out(c, ahead).wait_send()
                relay_on(c, ahead).wait_send()
    for forward in sent:
        forward.wait_send()
    own_feat.wait()
    for j, partner in enumerate(rep_partners, start=1):
        feat_copy(j, partner).wait()


def gather_sources(scaled, features, steps, blocks, group):
    slab_rows, width = scaled.shape
    plans = relay_plan(steps, blocks, group)
    return pl.pallas_call(
        functools.partial(gather_kernel, steps, blocks, plans, group),
        out_shape=(
            jax.ShapeDtypeStruct((steps, slab_rows, width), scaled.dtype),
            jax.ShapeDtypeStruct((group,) + features.shape, features.dtype),
        ),
        in_specs=[pl.BlockSpec(memory_space=pl.ANY)] * 2,
        out_specs=(pl.BlockSpec(memory_space=pl.ANY), pl.BlockSpec(memory_space=pl.ANY)),
        scratch_shapes=[
            pltpu.VMEM((CHUNKS, slab_rows // CHUNKS, width), scaled.dtype),
            pltpu.SemaphoreType.DMA((steps, CHUNKS)),
            pltpu.SemaphoreType.DMA((steps, CHUNKS)),
            pltpu.SemaphoreType.DMA((CHUNKS,)),
            pltpu.SemaphoreType.DMA((CHUNKS,)),
            pltpu.SemaphoreType.DMA((2, group)),
        ],
        compiler_params=pltpu.CompilerParams(collective_id=0, has_side_effects=True),
    )(scaled, features)


def finish_kernel(group, digits, partial_ref, root_ref, term_ref, weight_t_ref, grad_ref, out_ref,
                  sums_in, inbox, spread, gathered, sems):
    me = lax.axis_index("blk")
    rep = lax.axis_index("rep")
    share = grad_ref.shape[0]
    piece = out_ref.shape[0] // group
    rep_partners = [lax.rem(rep + j, group) for j in range(1, group)]
    barrier = pltpu.get_barrier_semaphore()
    for partner in rep_partners:
        pl.semaphore_signal(barrier, inc=1, device_id=(me, partner), device_id_type=MESH_ID)
    blk_count = 0
    for shift, width in digits:
        for d in range(1, 1 << width):
            pl.semaphore_signal(
                barrier, inc=1, device_id=(jnp.bitwise_xor(me, d << shift), rep), device_id_type=MESH_ID
            )
            blk_count += 1
    pl.semaphore_wait(barrier, group - 1 + blk_count)

    def send(src, dst, sem_row, slot, device):
        return pltpu.make_async_remote_copy(
            src_ref=src,
            dst_ref=dst,
            send_sem=sems.at[0, sem_row, slot],
            recv_sem=sems.at[1, sem_row, slot],
            device_id=device,
            device_id_type=MESH_ID,
        )

    first = []
    for j, partner in enumerate(rep_partners, start=1):
        rows = pl.ds(pl.multiple_of(partner * share, 8), share)
        first.append(send(partial_ref.at[rows], sums_in.at[j], 0, j, (me, partner)))
        rows = pl.ds(pl.multiple_of(partner * piece, 8), piece)
        first.append(send(term_ref.at[rows], inbox.at[j], 1, j, (me, partner)))
    for c in first:
        c.start()
    for c in first:
        c.wait()
    own_rows = pl.ds(pl.multiple_of(rep * share, 8), share)
    summed = partial_ref[own_rows].astype(jnp.float32)
    for j in range(1, group):
        summed = summed + sums_in[j].astype(jnp.float32)
    aggregated = (summed * root_ref[...]).astype(jnp.bfloat16)
    grad_ref[...] = jnp.dot(
        aggregated, weight_t_ref[...], preferred_element_type=jnp.float32
    ).astype(grad_ref.dtype)
    own = pl.ds(pl.multiple_of(rep * piece, 8), piece)
    total = term_ref[own]
    for j in range(1, group):
        total = total + inbox[j]
    spread[1, 0] = total

    for level, (shift, width) in enumerate(digits, start=1):
        members = 1 << width
        mine = jnp.bitwise_and(jnp.right_shift(me, shift), members - 1)
        swaps = [
            send(spread.at[level, 0], spread.at[level + 1, d], level + 1, d,
                 (jnp.bitwise_xor(me, d << shift), rep))
            for d in range(1, members)
        ]
        for c in swaps:
            c.start()
        for c in swaps:
            c.wait()
        spread[level + 1, 0] = spread[level, 0]
        total = spread[level + 1, mine]
        for i in range(1, members):
            total = total + spread[level + 1, jnp.bitwise_xor(mine, i)]
        spread[level + 1, 0] = total

    last = len(digits) + 1
    gathered[rep] = spread[last, 0]
    spreads = [
        send(spread.at[last, 0], gathered.at[rep], last + 1, j, (me, partner))
        for j, partner in enumerate(rep_partners, start=1)
    ]
    for c in spreads:
        c.start()
    for c in spreads:
        c.wait()
    for r in range(group):
        out_ref[pl.ds(r * piece, piece)] = gathered[r]


def finish(partial_sums, share_root, term, weight):
    group = lax.axis_size("rep")
    bits = lax.axis_size("blk").bit_length() - 1
    digits = [(shift, min(3, bits - shift)) for shift in range(0, bits, 3)]
    slab_rows, width = partial_sums.shape
    share = slab_rows // group
    fan = term.shape[0]
    piece = fan // group
    vmem = pl.BlockSpec(memory_space=pltpu.VMEM)
    return pl.pallas_call(
        functools.partial(finish_kernel, group, digits),
        out_shape=(
            jax.ShapeDtypeStruct((share, weight.shape[0]), jnp.bfloat16),
            jax.ShapeDtypeStruct(term.shape, jnp.float32),
        ),
        in_specs=[vmem] * 4,
        out_specs=(vmem, vmem),
        scratch_shapes=[
            pltpu.VMEM((group, share, width), partial_sums.dtype),
            pltpu.VMEM((group, piece, term.shape[1]), jnp.float32),
            pltpu.VMEM((len(digits) + 2, 8, piece, term.shape[1]), jnp.float32),
            pltpu.VMEM((group, piece, term.shape[1]), jnp.float32),
            pltpu.SemaphoreType.DMA((2, len(digits) + 3, 8)),
        ],
        compiler_params=pltpu.CompilerParams(collective_id=1, has_side_effects=True),
    )(partial_sums, share_root[:, None], term, weight.T)


def unpack_blocks(words):
    shifts = jnp.arange(8, dtype=jnp.int32)
    bit_values = jnp.bitwise_and(
        jnp.right_shift(words[..., :, None, :], shifts[:, None]), 1
    )
    return bit_values.reshape(words.shape[:-2] + (128, 128)).astype(jnp.bfloat16)


def per_device(features, out_grad, weight, block_words, block_coords, block_counts, degrees):
    slab_rows, width = out_grad.shape
    row_blocks = slab_rows // 128
    group_size = lax.axis_size("rep")
    blocks = lax.axis_size("blk")
    step_count = blocks // group_size
    rep_index = lax.axis_index("rep")
    inverse_root = lax.rsqrt(degrees.astype(jnp.float32))
    scaled = (out_grad.astype(jnp.float32) * inverse_root[:, None]).astype(jnp.bfloat16)

    sources, feature_slab = gather_sources(scaled, features, step_count, blocks, group_size)
    sources = sources.reshape(step_count, row_blocks, 128, width)
    coords = block_coords[0]
    slot_total = coords.shape[-1]
    picked = jnp.take_along_axis(sources, coords[:, 0, :, None, None], axis=1)
    transposed = unpack_blocks(block_words[0])
    contrib = jnp.einsum(
        "skvu,skuf->skvf", transposed, picked, preferred_element_type=jnp.float32
    )
    live = jnp.arange(slot_total, dtype=jnp.int32)[None, :] < block_counts[0][:, None]
    column_ids = jnp.arange(row_blocks, dtype=jnp.int32)
    placement = (
        (coords[:, 1, :, None] == column_ids[None, None, :]) & live[:, :, None]
    ).astype(jnp.float32)
    accumulated = jnp.einsum("skc,skvf->cvf", placement, contrib)

    partial_sums = accumulated.reshape(slab_rows, width)
    share_rows = slab_rows // group_size
    share_root = lax.dynamic_slice_in_dim(inverse_root, rep_index * share_rows, share_rows, 0)
    scaled_sums = (partial_sums * inverse_root[:, None]).astype(jnp.bfloat16)
    term = lax.dot_general(
        feature_slab.reshape(slab_rows, -1), scaled_sums, (((0,), (0,)), ((), ())),
        preferred_element_type=jnp.float32,
    )
    input_grad, weight_sum = finish(partial_sums.astype(jnp.bfloat16), share_root, term, weight)
    node_total = slab_rows * blocks
    weight_grad = weight_sum * (1.0 / math.sqrt(node_total))
    return (input_grad, weight_grad)


def solution(mesh):
    return jax.shard_map(
        per_device,
        mesh=mesh,
        in_specs=(
            P(("blk", "rep"), None),
            P("blk", None),
            P(),
            P("blk", "rep", None, None, None),
            P("blk", "rep", None, None),
            P("blk", "rep"),
            P("blk"),
        ),
        out_specs=(P(("blk", "rep"), None), P()),
        check_vma=False,
    )
```

```python
import functools
import math

import jax
import jax.numpy as jnp
from jax import lax
from jax.experimental import pallas as pl
from jax.experimental.pallas import tpu as pltpu
from jax.sharding import PartitionSpec as P

CHUNKS = 16
MESH_ID = pl.DeviceIdType.MESH


def relay_plan(steps, blocks, group):
    plans = []
    for rep in range(group):
        reach = steps * rep + steps // 2
        short = min(reach, blocks - reach)
        if 16 * short < 3 * blocks:
            plans.append((CHUNKS, 0, 0))
            continue
        direct = min(CHUNKS, max(1, int(CHUNKS * (blocks - short) / blocks + 0.5)))
        sign = 1 if reach < blocks - reach else -1
        plans.append((direct, sign, (blocks - short) // 2))
    return plans


def gather_kernel(steps, blocks, plans, group, slab_ref, feat_ref, out_ref, feats_ref, relay_buf,
                  send_sem, recv_sem, relay_in_sem, relay_fwd_sem, feat_sem):
    me = lax.axis_index("blk")
    rep = lax.axis_index("rep")
    rows = slab_ref.shape[0] // CHUNKS
    centre = steps // 2
    reach = steps * rep + centre
    far_to = lax.rem(me - reach + blocks * steps, blocks)
    far_from = lax.rem(me + reach, blocks)
    left = lax.rem(me + blocks - 1, blocks)
    right = lax.rem(me + 1, blocks)

    def part(c):
        return pl.ds(c * rows, rows)

    def copy(src_slot, dst_slot, c, target):
        src = slab_ref.at[part(c)] if src_slot is None else out_ref.at[src_slot, part(c)]
        return pltpu.make_async_remote_copy(
            src_ref=src,
            dst_ref=out_ref.at[dst_slot, part(c)],
            send_sem=send_sem.at[dst_slot, c],
            recv_sem=recv_sem.at[dst_slot, c],
            device_id=(target, rep),
            device_id_type=MESH_ID,
        )

    def relay_out(c, target):
        return pltpu.make_async_remote_copy(
            src_ref=slab_ref.at[part(c)],
            dst_ref=relay_buf.at[c],
            send_sem=send_sem.at[centre, c],
            recv_sem=relay_in_sem.at[c],
            device_id=(target, rep),
            device_id_type=MESH_ID,
        )

    def relay_on(c, target):
        return pltpu.make_async_remote_copy(
            src_ref=relay_buf.at[c],
            dst_ref=out_ref.at[centre, part(c)],
            send_sem=relay_fwd_sem.at[c],
            recv_sem=recv_sem.at[centre, c],
            device_id=(target, rep),
            device_id_type=MESH_ID,
        )

    rep_partners = [lax.rem(rep + j, group) for j in range(1, group)]

    def feat_copy(j, partner):
        return pltpu.make_async_remote_copy(
            src_ref=feat_ref,
            dst_ref=feats_ref.at[rep],
            send_sem=feat_sem.at[0, j],
            recv_sem=feat_sem.at[1, j],
            device_id=(me, partner),
            device_id_type=MESH_ID,
        )

    barrier = pltpu.get_barrier_semaphore()
    for partner in (left, right, far_to, far_from):
        pl.semaphore_signal(barrier, inc=1, device_id=(partner, rep), device_id_type=MESH_ID)
    for partner in rep_partners:
        pl.semaphore_signal(barrier, inc=1, device_id=(me, partner), device_id_type=MESH_ID)
    own_feat = pltpu.make_async_copy(feat_ref, feats_ref.at[rep], feat_sem.at[0, 0])
    own_feat.start()

    for plane, (direct, sign, leg) in enumerate(plans):
        @pl.when(rep == plane)
        def _():
            if direct < CHUNKS:
                ahead = lax.rem(me + sign * leg + blocks, blocks)
                behind = lax.rem(me - sign * leg + blocks, blocks)
                for partner in (ahead, behind):
                    pl.semaphore_signal(barrier, inc=1, device_id=(partner, rep), device_id_type=MESH_ID)
                pl.semaphore_wait(barrier, 6 + group - 1)
                for c in range(direct):
                    copy(None, centre, c, far_to).start()
                for j, partner in enumerate(rep_partners, start=1):
                    feat_copy(j, partner).start()
                for c in range(direct, CHUNKS):
                    relay_out(c, ahead).start()
                for c in range(direct, CHUNKS):
                    relay_out(c, ahead).wait_recv()
                    relay_on(c, ahead).start()
            else:
                pl.semaphore_wait(barrier, 4 + group - 1)
                for c in range(CHUNKS):
                    copy(None, centre, c, far_to).start()
                for j, partner in enumerate(rep_partners, start=1):
                    feat_copy(j, partner).start()

    sent = []
    for k in range(1, centre + 1):
        for c in range(CHUNKS):
            up = centre + k
            down = centre - k
            if up < steps:
                copy(up - 1, up - 1, c, left).wait_recv()
                forward = copy(up - 1, up, c, left)
                forward.start()
                sent.append(forward)
            if down >= 0:
                if k > 1 or up >= steps:
                    copy(down + 1, down + 1, c, right).wait_recv()
                forward = copy(down + 1, down, c, right)
                forward.start()
                sent.append(forward)

    for c in range(CHUNKS):
        copy(None, steps - 1, c, left).wait_recv()
        copy(None, 0, c, right).wait_recv()

    for plane, (direct, sign, leg) in enumerate(plans):
        @pl.when(rep == plane)
        def _():
            ahead = lax.rem(me + sign * leg + blocks, blocks)
            for c in range(direct):
                copy(None, centre, c, far_to).wait_send()
            for c in range(direct, CHUNKS):
                relay_out(c, ahead).wait_send()
                relay_on(c, ahead).wait_send()
    for forward in sent:
        forward.wait_send()
    own_feat.wait()
    for j, partner in enumerate(rep_partners, start=1):
        feat_copy(j, partner).wait()


def gather_sources(scaled, features, steps, blocks, group):
    slab_rows, width = scaled.shape
    plans = relay_plan(steps, blocks, group)
    return pl.pallas_call(
        functools.partial(gather_kernel, steps, blocks, plans, group),
        out_shape=(
            jax.ShapeDtypeStruct((steps, slab_rows, width), scaled.dtype),
            jax.ShapeDtypeStruct((group,) + features.shape, features.dtype),
        ),
        in_specs=[pl.BlockSpec(memory_space=pl.ANY)] * 2,
        out_specs=(pl.BlockSpec(memory_space=pl.ANY), pl.BlockSpec(memory_space=pl.ANY)),
        scratch_shapes=[
            pltpu.VMEM((CHUNKS, slab_rows // CHUNKS, width), scaled.dtype),
            pltpu.SemaphoreType.DMA((steps, CHUNKS)),
            pltpu.SemaphoreType.DMA((steps, CHUNKS)),
            pltpu.SemaphoreType.DMA((CHUNKS,)),
            pltpu.SemaphoreType.DMA((CHUNKS,)),
            pltpu.SemaphoreType.DMA((2, group)),
        ],
        compiler_params=pltpu.CompilerParams(collective_id=0, has_side_effects=True),
    )(scaled, features)


def finish_kernel(group, digits, partial_ref, root_ref, term_ref, weight_t_ref, grad_ref, out_ref,
                  sums_in, inbox, spread, gathered, sems):
    me = lax.axis_index("blk")
    rep = lax.axis_index("rep")
    share = grad_ref.shape[0]
    piece = out_ref.shape[0] // group
    rep_partners = [lax.rem(rep + j, group) for j in range(1, group)]
    barrier = pltpu.get_barrier_semaphore()
    for partner in rep_partners:
        pl.semaphore_signal(barrier, inc=1, device_id=(me, partner), device_id_type=MESH_ID)
    blk_count = 0
    for shift, width in digits:
        for d in range(1, 1 << width):
            pl.semaphore_signal(
                barrier, inc=1, device_id=(jnp.bitwise_xor(me, d << shift), rep), device_id_type=MESH_ID
            )
            blk_count += 1
    pl.semaphore_wait(barrier, group - 1 + blk_count)

    def send(src, dst, sem_row, slot, device):
        return pltpu.make_async_remote_copy(
            src_ref=src,
            dst_ref=dst,
            send_sem=sems.at[0, sem_row, slot],
            recv_sem=sems.at[1, sem_row, slot],
            device_id=device,
            device_id_type=MESH_ID,
        )

    first = []
    for j, partner in enumerate(rep_partners, start=1):
        rows = pl.ds(pl.multiple_of(partner * share, 8), share)
        first.append(send(partial_ref.at[rows], sums_in.at[j], 0, j, (me, partner)))
        rows = pl.ds(pl.multiple_of(partner * piece, 8), piece)
        first.append(send(term_ref.at[rows], inbox.at[j], 1, j, (me, partner)))
    for c in first:
        c.start()
    for c in first:
        c.wait()
    own_rows = pl.ds(pl.multiple_of(rep * share, 8), share)
    summed = partial_ref[own_rows].astype(jnp.float32)
    for j in range(1, group):
        summed = summed + sums_in[j].astype(jnp.float32)
    aggregated = (summed * root_ref[...]).astype(jnp.bfloat16)
    grad_ref[...] = jnp.dot(
        aggregated, weight_t_ref[...], preferred_element_type=jnp.float32
    ).astype(grad_ref.dtype)
    own = pl.ds(pl.multiple_of(rep * piece, 8), piece)
    total = term_ref[own]
    for j in range(1, group):
        total = total + inbox[j]
    spread[1, 0] = total

    for level, (shift, width) in enumerate(digits, start=1):
        members = 1 << width
        mine = jnp.bitwise_and(jnp.right_shift(me, shift), members - 1)
        swaps = [
            send(spread.at[level, 0], spread.at[level + 1, d], level + 1, d,
                 (jnp.bitwise_xor(me, d << shift), rep))
            for d in range(1, members)
        ]
        for c in swaps:
            c.start()
        for c in swaps:
            c.wait()
        spread[level + 1, 0] = spread[level, 0]
        total = spread[level + 1, mine]
        for i in range(1, members):
            total = total + spread[level + 1, jnp.bitwise_xor(mine, i)]
        spread[level + 1, 0] = total

    last = len(digits) + 1
    gathered[rep] = spread[last, 0]
    spreads = [
        send(spread.at[last, 0], gathered.at[rep], last + 1, j, (me, partner))
        for j, partner in enumerate(rep_partners, start=1)
    ]
    for c in spreads:
        c.start()
    for c in spreads:
        c.wait()
    for r in range(group):
        out_ref[pl.ds(r * piece, piece)] = gathered[r]


def finish(partial_sums, share_root, term, weight):
    group = lax.axis_size("rep")
    bits = lax.axis_size("blk").bit_length() - 1
    digits = [(shift, min(3, bits - shift)) for shift in range(0, bits, 3)]
    slab_rows, width = partial_sums.shape
    share = slab_rows // group
    fan = term.shape[0]
    piece = fan // group
    vmem = pl.BlockSpec(memory_space=pltpu.VMEM)
    return pl.pallas_call(
        functools.partial(finish_kernel, group, digits),
        out_shape=(
            jax.ShapeDtypeStruct((share, weight.shape[0]), jnp.bfloat16),
            jax.ShapeDtypeStruct(term.shape, jnp.float32),
        ),
        in_specs=[vmem] * 4,
        out_specs=(vmem, vmem),
        scratch_shapes=[
            pltpu.VMEM((group, share, width), partial_sums.dtype),
            pltpu.VMEM((group, piece, term.shape[1]), jnp.float32),
            pltpu.VMEM((len(digits) + 2, 8, piece, term.shape[1]), jnp.float32),
            pltpu.VMEM((group, piece, term.shape[1]), jnp.float32),
            pltpu.SemaphoreType.DMA((2, len(digits) + 3, 8)),
        ],
        compiler_params=pltpu.CompilerParams(collective_id=1, has_side_effects=True),
    )(partial_sums, share_root[:, None], term, weight.T)


def slot_kernel(slots, coords_ref, counts_ref, src_ref, words_ref, out_ref):
    s = pl.program_id(0)

    @pl.when(s == 0)
    def _():
        out_ref[...] = jnp.zeros_like(out_ref)

    shifts = lax.broadcasted_iota(jnp.int32, (1, 8, 1), 1)
    for k in range(slots):
        @pl.when(k < counts_ref[s])
        def _():
            p = coords_ref[s, 0, k]
            q = coords_ref[s, 1, k]
            picked = src_ref[0, pl.ds(pl.multiple_of(p * 128, 128), 128), :]
            words = words_ref[0, k]
            bits = jnp.bitwise_and(jnp.right_shift(words[:, None, :], shifts), 1)
            transposed = bits.reshape(128, 128).astype(jnp.bfloat16)
            rows = pl.ds(pl.multiple_of(q * 128, 128), 128)
            out_ref[rows, :] += jnp.dot(transposed, picked, preferred_element_type=jnp.float32)


def slot_sums(sources, words, coords, counts):
    steps, slab_rows, width = sources.shape
    slots = words.shape[1]
    grid_spec = pltpu.PrefetchScalarGridSpec(
        num_scalar_prefetch=2,
        grid=(steps,),
        in_specs=[
            pl.BlockSpec((1, slab_rows, width), lambda s, c, n: (s, 0, 0)),
            pl.BlockSpec((1,) + words.shape[1:], lambda s, c, n: (s, 0, 0, 0)),
        ],
        out_specs=pl.BlockSpec((slab_rows, width), lambda s, c, n: (0, 0)),
    )
    return pl.pallas_call(
        functools.partial(slot_kernel, slots),
        out_shape=jax.ShapeDtypeStruct((slab_rows, width), jnp.float32),
        grid_spec=grid_spec,
        compiler_params=pltpu.CompilerParams(dimension_semantics=("arbitrary",)),
    )(coords, counts, sources, words)


def per_device(features, out_grad, weight, block_words, block_coords, block_counts, degrees):
    slab_rows, width = out_grad.shape
    row_blocks = slab_rows // 128
    group_size = lax.axis_size("rep")
    blocks = lax.axis_size("blk")
    step_count = blocks // group_size
    rep_index = lax.axis_index("rep")
    inverse_root = lax.rsqrt(degrees.astype(jnp.float32))
    scaled = (out_grad.astype(jnp.float32) * inverse_root[:, None]).astype(jnp.bfloat16)

    sources, feature_slab = gather_sources(scaled, features, step_count, blocks, group_size)
    partial_sums = slot_sums(sources, block_words[0], block_coords[0], block_counts[0])
    share_rows = slab_rows // group_size
    share_root = lax.dynamic_slice_in_dim(inverse_root, rep_index * share_rows, share_rows, 0)
    scaled_sums = (partial_sums * inverse_root[:, None]).astype(jnp.bfloat16)
    term = lax.dot_general(
        feature_slab.reshape(slab_rows, -1), scaled_sums, (((0,), (0,)), ((), ())),
        preferred_element_type=jnp.float32,
    )
    input_grad, weight_sum = finish(partial_sums.astype(jnp.bfloat16), share_root, term, weight)
    node_total = slab_rows * blocks
    weight_grad = weight_sum * (1.0 / math.sqrt(node_total))
    return (input_grad, weight_grad)


def solution(mesh):
    return jax.shard_map(
        per_device,
        mesh=mesh,
        in_specs=(
            P(("blk", "rep"), None),
            P("blk", None),
            P(),
            P("blk", "rep", None, None, None),
            P("blk", "rep", None, None),
            P("blk", "rep"),
            P("blk"),
        ),
        out_specs=(P(("blk", "rep"), None), P()),
        check_vma=False,
    )
```

```python
import functools
import math

import jax
import jax.numpy as jnp
from jax import lax
from jax.experimental import pallas as pl
from jax.experimental.pallas import tpu as pltpu
from jax.sharding import PartitionSpec as P

CHUNKS = 16
MESH_ID = pl.DeviceIdType.MESH


def relay_plan(steps, blocks, group):
    plans = []
    for rep in range(group):
        reach = steps * rep + steps // 2
        short = min(reach, blocks - reach)
        if 16 * short < 3 * blocks:
            plans.append((CHUNKS, 0, 0))
            continue
        direct = min(CHUNKS, max(1, int(CHUNKS * (blocks - short) / blocks + 0.5)))
        sign = 1 if reach < blocks - reach else -1
        plans.append((direct, sign, (blocks - short) // 2))
    return plans


def gather_kernel(steps, blocks, plans, group, slab_ref, feat_ref, out_ref, feats_ref, relay_buf,
                  send_sem, recv_sem, relay_in_sem, relay_fwd_sem, feat_sem):
    me = lax.axis_index("blk")
    rep = lax.axis_index("rep")
    rows = slab_ref.shape[0] // CHUNKS
    centre = steps // 2
    reach = steps * rep + centre
    far_to = lax.rem(me - reach + blocks * steps, blocks)
    far_from = lax.rem(me + reach, blocks)
    left = lax.rem(me + blocks - 1, blocks)
    right = lax.rem(me + 1, blocks)

    def part(c):
        return pl.ds(c * rows, rows)

    def copy(src_slot, dst_slot, c, target):
        src = slab_ref.at[part(c)] if src_slot is None else out_ref.at[src_slot, part(c)]
        return pltpu.make_async_remote_copy(
            src_ref=src,
            dst_ref=out_ref.at[dst_slot, part(c)],
            send_sem=send_sem.at[dst_slot, c],
            recv_sem=recv_sem.at[dst_slot, c],
            device_id=(target, rep),
            device_id_type=MESH_ID,
        )

    def relay_out(c, target):
        return pltpu.make_async_remote_copy(
            src_ref=slab_ref.at[part(c)],
            dst_ref=relay_buf.at[c],
            send_sem=send_sem.at[centre, c],
            recv_sem=relay_in_sem.at[c],
            device_id=(target, rep),
            device_id_type=MESH_ID,
        )

    def relay_on(c, target):
        return pltpu.make_async_remote_copy(
            src_ref=relay_buf.at[c],
            dst_ref=out_ref.at[centre, part(c)],
            send_sem=relay_fwd_sem.at[c],
            recv_sem=recv_sem.at[centre, c],
            device_id=(target, rep),
            device_id_type=MESH_ID,
        )

    rep_partners = [lax.rem(rep + j, group) for j in range(1, group)]

    def feat_copy(j, partner):
        return pltpu.make_async_remote_copy(
            src_ref=feat_ref,
            dst_ref=feats_ref.at[rep],
            send_sem=feat_sem.at[0, j],
            recv_sem=feat_sem.at[1, j],
            device_id=(me, partner),
            device_id_type=MESH_ID,
        )

    barrier = pltpu.get_barrier_semaphore()
    for partner in (left, right, far_to, far_from):
        pl.semaphore_signal(barrier, inc=1, device_id=(partner, rep), device_id_type=MESH_ID)
    for partner in rep_partners:
        pl.semaphore_signal(barrier, inc=1, device_id=(me, partner), device_id_type=MESH_ID)
    own_feat = pltpu.make_async_copy(feat_ref, feats_ref.at[rep], feat_sem.at[0, 0])
    own_feat.start()

    for plane, (direct, sign, leg) in enumerate(plans):
        @pl.when(rep == plane)
        def _():
            if direct < CHUNKS:
                ahead = lax.rem(me + sign * leg + blocks, blocks)
                behind = lax.rem(me - sign * leg + blocks, blocks)
                for partner in (ahead, behind):
                    pl.semaphore_signal(barrier, inc=1, device_id=(partner, rep), device_id_type=MESH_ID)
                pl.semaphore_wait(barrier, 6 + group - 1)
                for c in range(direct):
                    copy(None, centre, c, far_to).start()
                for j, partner in enumerate(rep_partners, start=1):
                    feat_copy(j, partner).start()
                for c in range(direct, CHUNKS):
                    relay_out(c, ahead).start()
                for c in range(direct, CHUNKS):
                    relay_out(c, ahead).wait_recv()
                    relay_on(c, ahead).start()
            else:
                pl.semaphore_wait(barrier, 4 + group - 1)
                for c in range(CHUNKS):
                    copy(None, centre, c, far_to).start()
                for j, partner in enumerate(rep_partners, start=1):
                    feat_copy(j, partner).start()

    sent = []
    for k in range(1, centre + 1):
        for c in range(CHUNKS):
            up = centre + k
            down = centre - k
            if up < steps:
                copy(up - 1, up - 1, c, left).wait_recv()
                forward = copy(up - 1, up, c, left)
                forward.start()
                sent.append(forward)
            if down >= 0:
                if k > 1 or up >= steps:
                    copy(down + 1, down + 1, c, right).wait_recv()
                forward = copy(down + 1, down, c, right)
                forward.start()
                sent.append(forward)

    for c in range(CHUNKS):
        copy(None, steps - 1, c, left).wait_recv()
        copy(None, 0, c, right).wait_recv()

    for plane, (direct, sign, leg) in enumerate(plans):
        @pl.when(rep == plane)
        def _():
            ahead = lax.rem(me + sign * leg + blocks, blocks)
            for c in range(direct):
                copy(None, centre, c, far_to).wait_send()
            for c in range(direct, CHUNKS):
                relay_out(c, ahead).wait_send()
                relay_on(c, ahead).wait_send()
    for forward in sent:
        forward.wait_send()
    own_feat.wait()
    for j, partner in enumerate(rep_partners, start=1):
        feat_copy(j, partner).wait()


def gather_sources(scaled, features, steps, blocks, group):
    slab_rows, width = scaled.shape
    plans = relay_plan(steps, blocks, group)
    return pl.pallas_call(
        functools.partial(gather_kernel, steps, blocks, plans, group),
        out_shape=(
            jax.ShapeDtypeStruct((steps, slab_rows, width), scaled.dtype),
            jax.ShapeDtypeStruct((group,) + features.shape, features.dtype),
        ),
        in_specs=[pl.BlockSpec(memory_space=pl.ANY)] * 2,
        out_specs=(pl.BlockSpec(memory_space=pl.ANY), pl.BlockSpec(memory_space=pl.ANY)),
        scratch_shapes=[
            pltpu.VMEM((CHUNKS, slab_rows // CHUNKS, width), scaled.dtype),
            pltpu.SemaphoreType.DMA((steps, CHUNKS)),
            pltpu.SemaphoreType.DMA((steps, CHUNKS)),
            pltpu.SemaphoreType.DMA((CHUNKS,)),
            pltpu.SemaphoreType.DMA((CHUNKS,)),
            pltpu.SemaphoreType.DMA((2, group)),
        ],
        compiler_params=pltpu.CompilerParams(collective_id=0, has_side_effects=True),
    )(scaled, features)


def finish_kernel(group, digits, partial_ref, root_ref, feat_ref, scaled_ref, weight_t_ref, grad_ref,
                  out_ref, term_ref, sums_in, inbox, spread, gathered, sems):
    me = lax.axis_index("blk")
    rep = lax.axis_index("rep")
    share = grad_ref.shape[0]
    piece = out_ref.shape[0] // group
    rep_partners = [lax.rem(rep + j, group) for j in range(1, group)]
    barrier = pltpu.get_barrier_semaphore()
    for partner in rep_partners:
        pl.semaphore_signal(barrier, inc=1, device_id=(me, partner), device_id_type=MESH_ID)
    blk_count = 0
    for shift, width in digits:
        for d in range(1, 1 << width):
            pl.semaphore_signal(
                barrier, inc=1, device_id=(jnp.bitwise_xor(me, d << shift), rep), device_id_type=MESH_ID
            )
            blk_count += 1
    term_ref[...] = lax.dot_general(
        feat_ref[...], scaled_ref[...], (((0,), (0,)), ((), ())), preferred_element_type=jnp.float32
    )
    pl.semaphore_wait(barrier, group - 1 + blk_count)

    def send(src, dst, sem_row, slot, device):
        return pltpu.make_async_remote_copy(
            src_ref=src,
            dst_ref=dst,
            send_sem=sems.at[0, sem_row, slot],
            recv_sem=sems.at[1, sem_row, slot],
            device_id=device,
            device_id_type=MESH_ID,
        )

    first = []
    for j, partner in enumerate(rep_partners, start=1):
        rows = pl.ds(pl.multiple_of(partner * share, 8), share)
        first.append(send(partial_ref.at[rows], sums_in.at[j], 0, j, (me, partner)))
        rows = pl.ds(pl.multiple_of(partner * piece, 8), piece)
        first.append(send(term_ref.at[rows], inbox.at[j], 1, j, (me, partner)))
    for c in first:
        c.start()
    for c in first:
        c.wait()
    own_rows = pl.ds(pl.multiple_of(rep * share, 8), share)
    summed = partial_ref[own_rows].astype(jnp.float32)
    for j in range(1, group):
        summed = summed + sums_in[j].astype(jnp.float32)
    aggregated = (summed * root_ref[...]).astype(jnp.bfloat16)
    grad_ref[...] = jnp.dot(
        aggregated, weight_t_ref[...], preferred_element_type=jnp.float32
    ).astype(grad_ref.dtype)
    own = pl.ds(pl.multiple_of(rep * piece, 8), piece)
    total = term_ref[own]
    for j in range(1, group):
        total = total + inbox[j]
    spread[1, 0] = total

    for level, (shift, width) in enumerate(digits, start=1):
        members = 1 << width
        mine = jnp.bitwise_and(jnp.right_shift(me, shift), members - 1)
        swaps = [
            send(spread.at[level, 0], spread.at[level + 1, d], level + 1, d,
                 (jnp.bitwise_xor(me, d << shift), rep))
            for d in range(1, members)
        ]
        for c in swaps:
            c.start()
        for c in swaps:
            c.wait()
        spread[level + 1, 0] = spread[level, 0]
        total = spread[level + 1, mine]
        for i in range(1, members):
            total = total + spread[level + 1, jnp.bitwise_xor(mine, i)]
        spread[level + 1, 0] = total

    last = len(digits) + 1
    gathered[rep] = spread[last, 0]
    spreads = [
        send(spread.at[last, 0], gathered.at[rep], last + 1, j, (me, partner))
        for j, partner in enumerate(rep_partners, start=1)
    ]
    for c in spreads:
        c.start()
    for c in spreads:
        c.wait()
    for r in range(group):
        out_ref[pl.ds(r * piece, piece)] = gathered[r]


def finish(partial_sums, share_root, feature_slab, scaled_sums, weight):
    group = lax.axis_size("rep")
    bits = lax.axis_size("blk").bit_length() - 1
    digits = [(shift, min(3, bits - shift)) for shift in range(0, bits, 3)]
    slab_rows, width = partial_sums.shape
    share = slab_rows // group
    fan = feature_slab.shape[1]
    piece = fan // group
    vmem = pl.BlockSpec(memory_space=pltpu.VMEM)
    return pl.pallas_call(
        functools.partial(finish_kernel, group, digits),
        out_shape=(
            jax.ShapeDtypeStruct((share, weight.shape[0]), jnp.bfloat16),
            jax.ShapeDtypeStruct((fan, width), jnp.float32),
        ),
        in_specs=[vmem] * 5,
        out_specs=(vmem, vmem),
        scratch_shapes=[
            pltpu.VMEM((fan, width), jnp.float32),
            pltpu.VMEM((group, share, width), partial_sums.dtype),
            pltpu.VMEM((group, piece, width), jnp.float32),
            pltpu.VMEM((len(digits) + 2, 8, piece, width), jnp.float32),
            pltpu.VMEM((group, piece, width), jnp.float32),
            pltpu.SemaphoreType.DMA((2, len(digits) + 3, 8)),
        ],
        compiler_params=pltpu.CompilerParams(collective_id=1, has_side_effects=True),
    )(partial_sums, share_root[:, None], feature_slab, scaled_sums, weight.T)


def slot_kernel(slots, coords_ref, counts_ref, src_ref, words_ref, root_ref, out_ref, sums_ref,
                scaled_ref):
    s = pl.program_id(0)

    @pl.when(s == 0)
    def _():
        out_ref[...] = jnp.zeros_like(out_ref)

    shifts = lax.broadcasted_iota(jnp.int32, (1, 8, 1), 1)
    for k in range(slots):
        @pl.when(k < counts_ref[s])
        def _():
            p = coords_ref[s, 0, k]
            q = coords_ref[s, 1, k]
            picked = src_ref[0, pl.ds(pl.multiple_of(p * 128, 128), 128), :]
            words = words_ref[0, k]
            bits = jnp.bitwise_and(jnp.right_shift(words[:, None, :], shifts), 1)
            transposed = bits.reshape(128, 128).astype(jnp.bfloat16)
            rows = pl.ds(pl.multiple_of(q * 128, 128), 128)
            out_ref[rows, :] += jnp.dot(transposed, picked, preferred_element_type=jnp.float32)

    @pl.when(s == pl.num_programs(0) - 1)
    def _():
        sums_ref[...] = out_ref[...].astype(sums_ref.dtype)
        scaled_ref[...] = (out_ref[...] * root_ref[...]).astype(scaled_ref.dtype)


def slot_sums(sources, words, coords, counts, inverse_root):
    steps, slab_rows, width = sources.shape
    slots = words.shape[1]
    grid_spec = pltpu.PrefetchScalarGridSpec(
        num_scalar_prefetch=2,
        grid=(steps,),
        in_specs=[
            pl.BlockSpec((1, slab_rows, width), lambda s, c, n: (s, 0, 0)),
            pl.BlockSpec((1,) + words.shape[1:], lambda s, c, n: (s, 0, 0, 0)),
            pl.BlockSpec((slab_rows, 1), lambda s, c, n: (0, 0)),
        ],
        out_specs=[
            pl.BlockSpec((slab_rows, width), lambda s, c, n: (0, 0)),
            pl.BlockSpec((slab_rows, width), lambda s, c, n: (0, 0)),
            pl.BlockSpec((slab_rows, width), lambda s, c, n: (0, 0)),
        ],
    )
    _, sums, scaled_sums = pl.pallas_call(
        functools.partial(slot_kernel, slots),
        out_shape=[
            jax.ShapeDtypeStruct((slab_rows, width), jnp.float32),
            jax.ShapeDtypeStruct((slab_rows, width), jnp.bfloat16),
            jax.ShapeDtypeStruct((slab_rows, width), jnp.bfloat16),
        ],
        grid_spec=grid_spec,
        compiler_params=pltpu.CompilerParams(dimension_semantics=("arbitrary",)),
    )(coords, counts, sources, words, inverse_root[:, None])
    return sums, scaled_sums


def per_device(features, out_grad, weight, block_words, block_coords, block_counts, degrees):
    slab_rows, width = out_grad.shape
    row_blocks = slab_rows // 128
    group_size = lax.axis_size("rep")
    blocks = lax.axis_size("blk")
    step_count = blocks // group_size
    rep_index = lax.axis_index("rep")
    inverse_root = lax.rsqrt(degrees.astype(jnp.float32))
    scaled = (out_grad.astype(jnp.float32) * inverse_root[:, None]).astype(jnp.bfloat16)

    sources, feature_slab = gather_sources(scaled, features, step_count, blocks, group_size)
    partial_sums, scaled_sums = slot_sums(
        sources, block_words[0], block_coords[0], block_counts[0], inverse_root
    )
    share_rows = slab_rows // group_size
    share_root = lax.dynamic_slice_in_dim(inverse_root, rep_index * share_rows, share_rows, 0)
    input_grad, weight_sum = finish(
        partial_sums, share_root, feature_slab.reshape(slab_rows, -1), scaled_sums, weight
    )
    node_total = slab_rows * blocks
    weight_grad = weight_sum * (1.0 / math.sqrt(node_total))
    return (input_grad, weight_grad)


def solution(mesh):
    return jax.shard_map(
        per_device,
        mesh=mesh,
        in_specs=(
            P(("blk", "rep"), None),
            P("blk", None),
            P(),
            P("blk", "rep", None, None, None),
            P("blk", "rep", None, None),
            P("blk", "rep"),
            P("blk"),
        ),
        out_specs=(P(("blk", "rep"), None), P()),
        check_vma=False,
    )
```

```python
import functools
import math

import jax
import jax.numpy as jnp
from jax import lax
from jax.experimental import pallas as pl
from jax.experimental.pallas import tpu as pltpu
from jax.sharding import PartitionSpec as P

CHUNKS = 16
MESH_ID = pl.DeviceIdType.MESH


def relay_plan(steps, blocks, group):
    plans = []
    for rep in range(group):
        reach = steps * rep + steps // 2
        short = min(reach, blocks - reach)
        if 16 * short < 3 * blocks:
            plans.append((CHUNKS, 0, 0))
            continue
        direct = min(CHUNKS, max(1, int(CHUNKS * (blocks - short) / blocks + 0.5)))
        sign = 1 if reach < blocks - reach else -1
        plans.append((direct, sign, (blocks - short) // 2))
    return plans


def gather_kernel(steps, blocks, plans, group, slab_ref, feat_ref, out_ref, feats_ref, relay_buf,
                  send_sem, recv_sem, relay_in_sem, relay_fwd_sem, feat_sem):
    me = lax.axis_index("blk")
    rep = lax.axis_index("rep")
    rows = slab_ref.shape[0] // CHUNKS
    centre = steps // 2
    reach = steps * rep + centre
    far_to = lax.rem(me - reach + blocks * steps, blocks)
    far_from = lax.rem(me + reach, blocks)
    left = lax.rem(me + blocks - 1, blocks)
    right = lax.rem(me + 1, blocks)

    def part(c):
        return pl.ds(c * rows, rows)

    def copy(src_slot, dst_slot, c, target):
        src = slab_ref.at[part(c)] if src_slot is None else out_ref.at[src_slot, part(c)]
        return pltpu.make_async_remote_copy(
            src_ref=src,
            dst_ref=out_ref.at[dst_slot, part(c)],
            send_sem=send_sem.at[dst_slot, c],
            recv_sem=recv_sem.at[dst_slot, c],
            device_id=(target, rep),
            device_id_type=MESH_ID,
        )

    def relay_out(c, target):
        return pltpu.make_async_remote_copy(
            src_ref=slab_ref.at[part(c)],
            dst_ref=relay_buf.at[c],
            send_sem=send_sem.at[centre, c],
            recv_sem=relay_in_sem.at[c],
            device_id=(target, rep),
            device_id_type=MESH_ID,
        )

    def relay_on(c, target):
        return pltpu.make_async_remote_copy(
            src_ref=relay_buf.at[c],
            dst_ref=out_ref.at[centre, part(c)],
            send_sem=relay_fwd_sem.at[c],
            recv_sem=recv_sem.at[centre, c],
            device_id=(target, rep),
            device_id_type=MESH_ID,
        )

    rep_partners = [lax.rem(rep + j, group) for j in range(1, group)]

    def feat_copy(j, partner):
        return pltpu.make_async_remote_copy(
            src_ref=feat_ref,
            dst_ref=feats_ref.at[rep],
            send_sem=feat_sem.at[0, j],
            recv_sem=feat_sem.at[1, j],
            device_id=(me, partner),
            device_id_type=MESH_ID,
        )

    barrier = pltpu.get_barrier_semaphore()
    for partner in (left, right, far_to, far_from):
        pl.semaphore_signal(barrier, inc=1, device_id=(partner, rep), device_id_type=MESH_ID)
    for partner in rep_partners:
        pl.semaphore_signal(barrier, inc=1, device_id=(me, partner), device_id_type=MESH_ID)
    own_feat = pltpu.make_async_copy(feat_ref, feats_ref.at[rep], feat_sem.at[0, 0])
    own_feat.start()

    for plane, (direct, sign, leg) in enumerate(plans):
        @pl.when(rep == plane)
        def _():
            if direct < CHUNKS:
                ahead = lax.rem(me + sign * leg + blocks, blocks)
                behind = lax.rem(me - sign * leg + blocks, blocks)
                for partner in (ahead, behind):
                    pl.semaphore_signal(barrier, inc=1, device_id=(partner, rep), device_id_type=MESH_ID)
                pl.semaphore_wait(barrier, 6 + group - 1)
                for c in range(direct):
                    copy(None, centre, c, far_to).start()
                for j, partner in enumerate(rep_partners, start=1):
                    feat_copy(j, partner).start()
                for c in range(direct, CHUNKS):
                    relay_out(c, ahead).start()
            else:
                pl.semaphore_wait(barrier, 4 + group - 1)
                for c in range(CHUNKS):
                    copy(None, centre, c, far_to).start()
                for j, partner in enumerate(rep_partners, start=1):
                    feat_copy(j, partner).start()

    sent = []
    for k in range(1, centre + 1):
        for c in range(CHUNKS):
            if k == 1:
                for plane, (direct, sign, leg) in enumerate(plans):
                    if c >= direct:
                        @pl.when(rep == plane)
                        def _():
                            ahead = lax.rem(me + sign * leg + blocks, blocks)
                            relay_out(c, ahead).wait_recv()
                            relay_on(c, ahead).start()
            up = centre + k
            down = centre - k
            if up < steps:
                copy(up - 1, up - 1, c, left).wait_recv()
                forward = copy(up - 1, up, c, left)
                forward.start()
                sent.append(forward)
            if down >= 0:
                if k > 1 or up >= steps:
                    copy(down + 1, down + 1, c, right).wait_recv()
                forward = copy(down + 1, down, c, right)
                forward.start()
                sent.append(forward)

    for c in range(CHUNKS):
        copy(None, steps - 1, c, left).wait_recv()
        copy(None, 0, c, right).wait_recv()

    for plane, (direct, sign, leg) in enumerate(plans):
        @pl.when(rep == plane)
        def _():
            ahead = lax.rem(me + sign * leg + blocks, blocks)
            for c in range(direct):
                copy(None, centre, c, far_to).wait_send()
            for c in range(direct, CHUNKS):
                relay_out(c, ahead).wait_send()
                relay_on(c, ahead).wait_send()
    for forward in sent:
        forward.wait_send()
    own_feat.wait()
    for j, partner in enumerate(rep_partners, start=1):
        feat_copy(j, partner).wait()


def gather_sources(scaled, features, steps, blocks, group):
    slab_rows, width = scaled.shape
    plans = relay_plan(steps, blocks, group)
    return pl.pallas_call(
        functools.partial(gather_kernel, steps, blocks, plans, group),
        out_shape=(
            jax.ShapeDtypeStruct((steps, slab_rows, width), scaled.dtype),
            jax.ShapeDtypeStruct((group,) + features.shape, features.dtype),
        ),
        in_specs=[pl.BlockSpec(memory_space=pl.ANY)] * 2,
        out_specs=(pl.BlockSpec(memory_space=pl.ANY), pl.BlockSpec(memory_space=pl.ANY)),
        scratch_shapes=[
            pltpu.VMEM((CHUNKS, slab_rows // CHUNKS, width), scaled.dtype),
            pltpu.SemaphoreType.DMA((steps, CHUNKS)),
            pltpu.SemaphoreType.DMA((steps, CHUNKS)),
            pltpu.SemaphoreType.DMA((CHUNKS,)),
            pltpu.SemaphoreType.DMA((CHUNKS,)),
            pltpu.SemaphoreType.DMA((2, group)),
        ],
        compiler_params=pltpu.CompilerParams(collective_id=0, has_side_effects=True),
    )(scaled, features)


def finish_kernel(group, digits, partial_ref, root_ref, feat_ref, scaled_ref, weight_t_ref, grad_ref,
                  out_ref, term_ref, sums_in, inbox, spread, gathered, sems):
    me = lax.axis_index("blk")
    rep = lax.axis_index("rep")
    share = grad_ref.shape[0]
    piece = out_ref.shape[0] // group
    rep_partners = [lax.rem(rep + j, group) for j in range(1, group)]
    barrier = pltpu.get_barrier_semaphore()
    for partner in rep_partners:
        pl.semaphore_signal(barrier, inc=1, device_id=(me, partner), device_id_type=MESH_ID)
    blk_count = 0
    for shift, width in digits:
        for d in range(1, 1 << width):
            pl.semaphore_signal(
                barrier, inc=1, device_id=(jnp.bitwise_xor(me, d << shift), rep), device_id_type=MESH_ID
            )
            blk_count += 1
    term_ref[...] = lax.dot_general(
        feat_ref[...], scaled_ref[...], (((0,), (0,)), ((), ())), preferred_element_type=jnp.float32
    )
    pl.semaphore_wait(barrier, group - 1 + blk_count)

    def send(src, dst, sem_row, slot, device):
        return pltpu.make_async_remote_copy(
            src_ref=src,
            dst_ref=dst,
            send_sem=sems.at[0, sem_row, slot],
            recv_sem=sems.at[1, sem_row, slot],
            device_id=device,
            device_id_type=MESH_ID,
        )

    first = []
    for j, partner in enumerate(rep_partners, start=1):
        rows = pl.ds(pl.multiple_of(partner * share, 8), share)
        first.append(send(partial_ref.at[rows], sums_in.at[j], 0, j, (me, partner)))
        rows = pl.ds(pl.multiple_of(partner * piece, 8), piece)
        first.append(send(term_ref.at[rows], inbox.at[j], 1, j, (me, partner)))
    for c in first:
        c.start()
    for c in first:
        c.wait()
    own_rows = pl.ds(pl.multiple_of(rep * share, 8), share)
    summed = partial_ref[own_rows].astype(jnp.float32)
    for j in range(1, group):
        summed = summed + sums_in[j].astype(jnp.float32)
    aggregated = (summed * root_ref[...]).astype(jnp.bfloat16)
    grad_ref[...] = jnp.dot(
        aggregated, weight_t_ref[...], preferred_element_type=jnp.float32
    ).astype(grad_ref.dtype)
    own = pl.ds(pl.multiple_of(rep * piece, 8), piece)
    total = term_ref[own]
    for j in range(1, group):
        total = total + inbox[j]
    spread[1, 0] = total

    for level, (shift, width) in enumerate(digits, start=1):
        members = 1 << width
        mine = jnp.bitwise_and(jnp.right_shift(me, shift), members - 1)
        swaps = [
            send(spread.at[level, 0], spread.at[level + 1, d], level + 1, d,
                 (jnp.bitwise_xor(me, d << shift), rep))
            for d in range(1, members)
        ]
        for c in swaps:
            c.start()
        for c in swaps:
            c.wait()
        spread[level + 1, 0] = spread[level, 0]
        total = spread[level + 1, mine]
        for i in range(1, members):
            total = total + spread[level + 1, jnp.bitwise_xor(mine, i)]
        spread[level + 1, 0] = total

    last = len(digits) + 1
    gathered[rep] = spread[last, 0]
    spreads = [
        send(spread.at[last, 0], gathered.at[rep], last + 1, j, (me, partner))
        for j, partner in enumerate(rep_partners, start=1)
    ]
    for c in spreads:
        c.start()
    for c in spreads:
        c.wait()
    for r in range(group):
        out_ref[pl.ds(r * piece, piece)] = gathered[r]


def finish(partial_sums, share_root, feature_slab, scaled_sums, weight):
    group = lax.axis_size("rep")
    bits = lax.axis_size("blk").bit_length() - 1
    digits = [(shift, min(3, bits - shift)) for shift in range(0, bits, 3)]
    slab_rows, width = partial_sums.shape
    share = slab_rows // group
    fan = feature_slab.shape[1]
    piece = fan // group
    vmem = pl.BlockSpec(memory_space=pltpu.VMEM)
    return pl.pallas_call(
        functools.partial(finish_kernel, group, digits),
        out_shape=(
            jax.ShapeDtypeStruct((share, weight.shape[0]), jnp.bfloat16),
            jax.ShapeDtypeStruct((fan, width), jnp.float32),
        ),
        in_specs=[vmem] * 5,
        out_specs=(vmem, vmem),
        scratch_shapes=[
            pltpu.VMEM((fan, width), jnp.float32),
            pltpu.VMEM((group, share, width), partial_sums.dtype),
            pltpu.VMEM((group, piece, width), jnp.float32),
            pltpu.VMEM((len(digits) + 2, 8, piece, width), jnp.float32),
            pltpu.VMEM((group, piece, width), jnp.float32),
            pltpu.SemaphoreType.DMA((2, len(digits) + 3, 8)),
        ],
        compiler_params=pltpu.CompilerParams(collective_id=1, has_side_effects=True),
    )(partial_sums, share_root[:, None], feature_slab, scaled_sums, weight.T)


def slot_kernel(slots, coords_ref, counts_ref, src_ref, words_ref, root_ref, out_ref, sums_ref,
                scaled_ref):
    s = pl.program_id(0)

    @pl.when(s == 0)
    def _():
        out_ref[...] = jnp.zeros_like(out_ref)

    shifts = lax.broadcasted_iota(jnp.int32, (1, 8, 1), 1)
    for k in range(slots):
        @pl.when(k < counts_ref[s])
        def _():
            p = coords_ref[s, 0, k]
            q = coords_ref[s, 1, k]
            picked = src_ref[0, pl.ds(pl.multiple_of(p * 128, 128), 128), :]
            words = words_ref[0, k]
            bits = jnp.bitwise_and(jnp.right_shift(words[:, None, :], shifts), 1)
            transposed = bits.reshape(128, 128).astype(jnp.bfloat16)
            rows = pl.ds(pl.multiple_of(q * 128, 128), 128)
            out_ref[rows, :] += jnp.dot(transposed, picked, preferred_element_type=jnp.float32)

    @pl.when(s == pl.num_programs(0) - 1)
    def _():
        sums_ref[...] = out_ref[...].astype(sums_ref.dtype)
        scaled_ref[...] = (out_ref[...] * root_ref[...]).astype(scaled_ref.dtype)


def slot_sums(sources, words, coords, counts, inverse_root):
    steps, slab_rows, width = sources.shape
    slots = words.shape[1]
    grid_spec = pltpu.PrefetchScalarGridSpec(
        num_scalar_prefetch=2,
        grid=(steps,),
        in_specs=[
            pl.BlockSpec((1, slab_rows, width), lambda s, c, n: (s, 0, 0)),
            pl.BlockSpec((1,) + words.shape[1:], lambda s, c, n: (s, 0, 0, 0)),
            pl.BlockSpec((slab_rows, 1), lambda s, c, n: (0, 0)),
        ],
        out_specs=[
            pl.BlockSpec((slab_rows, width), lambda s, c, n: (0, 0)),
            pl.BlockSpec((slab_rows, width), lambda s, c, n: (0, 0)),
            pl.BlockSpec((slab_rows, width), lambda s, c, n: (0, 0)),
        ],
    )
    _, sums, scaled_sums = pl.pallas_call(
        functools.partial(slot_kernel, slots),
        out_shape=[
            jax.ShapeDtypeStruct((slab_rows, width), jnp.float32),
            jax.ShapeDtypeStruct((slab_rows, width), jnp.bfloat16),
            jax.ShapeDtypeStruct((slab_rows, width), jnp.bfloat16),
        ],
        grid_spec=grid_spec,
        compiler_params=pltpu.CompilerParams(dimension_semantics=("arbitrary",)),
    )(coords, counts, sources, words, inverse_root[:, None])
    return sums, scaled_sums


def per_device(features, out_grad, weight, block_words, block_coords, block_counts, degrees):
    slab_rows, width = out_grad.shape
    row_blocks = slab_rows // 128
    group_size = lax.axis_size("rep")
    blocks = lax.axis_size("blk")
    step_count = blocks // group_size
    rep_index = lax.axis_index("rep")
    inverse_root = lax.rsqrt(degrees.astype(jnp.float32))
    scaled = (out_grad.astype(jnp.float32) * inverse_root[:, None]).astype(jnp.bfloat16)

    sources, feature_slab = gather_sources(scaled, features, step_count, blocks, group_size)
    partial_sums, scaled_sums = slot_sums(
        sources, block_words[0], block_coords[0], block_counts[0], inverse_root
    )
    share_rows = slab_rows // group_size
    share_root = lax.dynamic_slice_in_dim(inverse_root, rep_index * share_rows, share_rows, 0)
    input_grad, weight_sum = finish(
        partial_sums, share_root, feature_slab.reshape(slab_rows, -1), scaled_sums, weight
    )
    node_total = slab_rows * blocks
    weight_grad = weight_sum * (1.0 / math.sqrt(node_total))
    return (input_grad, weight_grad)


def solution(mesh):
    return jax.shard_map(
        per_device,
        mesh=mesh,
        in_specs=(
            P(("blk", "rep"), None),
            P("blk", None),
            P(),
            P("blk", "rep", None, None, None),
            P("blk", "rep", None, None),
            P("blk", "rep"),
            P("blk"),
        ),
        out_specs=(P(("blk", "rep"), None), P()),
        check_vma=False,
    )
```

```python
import functools
import math

import jax
import jax.numpy as jnp
from jax import lax
from jax.experimental import pallas as pl
from jax.experimental.pallas import tpu as pltpu
from jax.sharding import PartitionSpec as P

CHUNKS = 8
MESH_ID = pl.DeviceIdType.MESH


def relay_plan(steps, blocks, group):
    plans = []
    for rep in range(group):
        reach = steps * rep + steps // 2
        short = min(reach, blocks - reach)
        if 4 * short < 5 * blocks // 4:
            plans.append((CHUNKS, 0, 0))
            continue
        direct = min(CHUNKS, max(1, int(CHUNKS * (blocks - short) / blocks + 0.5)))
        sign = 1 if reach < blocks - reach else -1
        plans.append((direct, sign, (blocks - short) // 2))
    return plans


def gather_kernel(steps, blocks, plans, group, slab_ref, feat_ref, out_ref, feats_ref, relay_buf,
                  send_sem, recv_sem, relay_in_sem, relay_fwd_sem, feat_sem):
    me = lax.axis_index("blk")
    rep = lax.axis_index("rep")
    rows = slab_ref.shape[0] // CHUNKS
    centre = steps // 2
    reach = steps * rep + centre
    far_to = lax.rem(me - reach + blocks * steps, blocks)
    far_from = lax.rem(me + reach, blocks)
    left = lax.rem(me + blocks - 1, blocks)
    right = lax.rem(me + 1, blocks)

    def part(c):
        return pl.ds(c * rows, rows)

    def copy(src_slot, dst_slot, c, target):
        src = slab_ref.at[part(c)] if src_slot is None else out_ref.at[src_slot, part(c)]
        return pltpu.make_async_remote_copy(
            src_ref=src,
            dst_ref=out_ref.at[dst_slot, part(c)],
            send_sem=send_sem.at[dst_slot, c],
            recv_sem=recv_sem.at[dst_slot, c],
            device_id=(target, rep),
            device_id_type=MESH_ID,
        )

    def relay_out(c, target):
        return pltpu.make_async_remote_copy(
            src_ref=slab_ref.at[part(c)],
            dst_ref=relay_buf.at[c],
            send_sem=send_sem.at[centre, c],
            recv_sem=relay_in_sem.at[c],
            device_id=(target, rep),
            device_id_type=MESH_ID,
        )

    def relay_on(c, target):
        return pltpu.make_async_remote_copy(
            src_ref=relay_buf.at[c],
            dst_ref=out_ref.at[centre, part(c)],
            send_sem=relay_fwd_sem.at[c],
            recv_sem=recv_sem.at[centre, c],
            device_id=(target, rep),
            device_id_type=MESH_ID,
        )

    rep_partners = [lax.rem(rep + j, group) for j in range(1, group)]

    def feat_copy(j, partner):
        return pltpu.make_async_remote_copy(
            src_ref=feat_ref,
            dst_ref=feats_ref.at[rep],
            send_sem=feat_sem.at[0, j],
            recv_sem=feat_sem.at[1, j],
            device_id=(me, partner),
            device_id_type=MESH_ID,
        )

    barrier = pltpu.get_barrier_semaphore()
    for partner in (left, right, far_to, far_from):
        pl.semaphore_signal(barrier, inc=1, device_id=(partner, rep), device_id_type=MESH_ID)
    for partner in rep_partners:
        pl.semaphore_signal(barrier, inc=1, device_id=(me, partner), device_id_type=MESH_ID)
    own_feat = pltpu.make_async_copy(feat_ref, feats_ref.at[rep], feat_sem.at[0, 0])
    own_feat.start()

    for plane, (direct, sign, leg) in enumerate(plans):
        @pl.when(rep == plane)
        def _():
            if direct < CHUNKS:
                ahead = lax.rem(me + sign * leg + blocks, blocks)
                behind = lax.rem(me - sign * leg + blocks, blocks)
                for partner in (ahead, behind):
                    pl.semaphore_signal(barrier, inc=1, device_id=(partner, rep), device_id_type=MESH_ID)
                pl.semaphore_wait(barrier, 6 + group - 1)
                for c in range(direct):
                    copy(None, centre, c, far_to).start()
                for j, partner in enumerate(rep_partners, start=1):
                    feat_copy(j, partner).start()
                for c in range(direct, CHUNKS):
                    relay_out(c, ahead).start()
                for c in range(direct, CHUNKS):
                    relay_out(c, ahead).wait_recv()
                    relay_on(c, ahead).start()
            else:
                pl.semaphore_wait(barrier, 4 + group - 1)
                for c in range(CHUNKS):
                    copy(None, centre, c, far_to).start()
                for j, partner in enumerate(rep_partners, start=1):
                    feat_copy(j, partner).start()

    sent = []
    for k in range(1, centre + 1):
        for c in range(CHUNKS):
            up = centre + k
            down = centre - k
            if up < steps:
                copy(up - 1, up - 1, c, left).wait_recv()
                forward = copy(up - 1, up, c, left)
                forward.start()
                sent.append(forward)
            if down >= 0:
                if k > 1 or up >= steps:
                    copy(down + 1, down + 1, c, right).wait_recv()
                forward = copy(down + 1, down, c, right)
                forward.start()
                sent.append(forward)

    for c in range(CHUNKS):
        copy(None, steps - 1, c, left).wait_recv()
        copy(None, 0, c, right).wait_recv()

    for plane, (direct, sign, leg) in enumerate(plans):
        @pl.when(rep == plane)
        def _():
            ahead = lax.rem(me + sign * leg + blocks, blocks)
            for c in range(direct):
                copy(None, centre, c, far_to).wait_send()
            for c in range(direct, CHUNKS):
                relay_out(c, ahead).wait_send()
                relay_on(c, ahead).wait_send()
    for forward in sent:
        forward.wait_send()
    own_feat.wait()
    for j, partner in enumerate(rep_partners, start=1):
        feat_copy(j, partner).wait()


def gather_sources(scaled, features, steps, blocks, group):
    slab_rows, width = scaled.shape
    plans = relay_plan(steps, blocks, group)
    return pl.pallas_call(
        functools.partial(gather_kernel, steps, blocks, plans, group),
        out_shape=(
            jax.ShapeDtypeStruct((steps, slab_rows, width), scaled.dtype),
            jax.ShapeDtypeStruct((group,) + features.shape, features.dtype),
        ),
        in_specs=[pl.BlockSpec(memory_space=pl.ANY)] * 2,
        out_specs=(pl.BlockSpec(memory_space=pl.ANY), pl.BlockSpec(memory_space=pl.ANY)),
        scratch_shapes=[
            pltpu.VMEM((CHUNKS, slab_rows // CHUNKS, width), scaled.dtype),
            pltpu.SemaphoreType.DMA((steps, CHUNKS)),
            pltpu.SemaphoreType.DMA((steps, CHUNKS)),
            pltpu.SemaphoreType.DMA((CHUNKS,)),
            pltpu.SemaphoreType.DMA((CHUNKS,)),
            pltpu.SemaphoreType.DMA((2, group)),
        ],
        compiler_params=pltpu.CompilerParams(collective_id=0, has_side_effects=True),
    )(scaled, features)


def finish_kernel(group, digits, partial_ref, root_ref, feat_ref, scaled_ref, weight_t_ref, grad_ref,
                  out_ref, term_ref, sums_in, inbox, spread, gathered, sems):
    me = lax.axis_index("blk")
    rep = lax.axis_index("rep")
    share = grad_ref.shape[0]
    piece = out_ref.shape[0] // group
    rep_partners = [lax.rem(rep + j, group) for j in range(1, group)]
    barrier = pltpu.get_barrier_semaphore()
    for partner in rep_partners:
        pl.semaphore_signal(barrier, inc=1, device_id=(me, partner), device_id_type=MESH_ID)
    blk_count = 0
    for shift, width in digits:
        for d in range(1, 1 << width):
            pl.semaphore_signal(
                barrier, inc=1, device_id=(jnp.bitwise_xor(me, d << shift), rep), device_id_type=MESH_ID
            )
            blk_count += 1
    term_ref[...] = lax.dot_general(
        feat_ref[...], scaled_ref[...], (((0,), (0,)), ((), ())), preferred_element_type=jnp.float32
    )
    pl.semaphore_wait(barrier, group - 1 + blk_count)

    def send(src, dst, sem_row, slot, device):
        return pltpu.make_async_remote_copy(
            src_ref=src,
            dst_ref=dst,
            send_sem=sems.at[0, sem_row, slot],
            recv_sem=sems.at[1, sem_row, slot],
            device_id=device,
            device_id_type=MESH_ID,
        )

    first = []
    for j, partner in enumerate(rep_partners, start=1):
        rows = pl.ds(pl.multiple_of(partner * share, 8), share)
        first.append(send(partial_ref.at[rows], sums_in.at[j], 0, j, (me, partner)))
        rows = pl.ds(pl.multiple_of(partner * piece, 8), piece)
        first.append(send(term_ref.at[rows], inbox.at[j], 1, j, (me, partner)))
    for c in first:
        c.start()
    for c in first:
        c.wait()
    own_rows = pl.ds(pl.multiple_of(rep * share, 8), share)
    summed = partial_ref[own_rows].astype(jnp.float32)
    for j in range(1, group):
        summed = summed + sums_in[j].astype(jnp.float32)
    aggregated = (summed * root_ref[...]).astype(jnp.bfloat16)
    grad_ref[...] = jnp.dot(
        aggregated, weight_t_ref[...], preferred_element_type=jnp.float32
    ).astype(grad_ref.dtype)
    own = pl.ds(pl.multiple_of(rep * piece, 8), piece)
    total = term_ref[own]
    for j in range(1, group):
        total = total + inbox[j]
    spread[1, 0] = total

    for level, (shift, width) in enumerate(digits, start=1):
        members = 1 << width
        mine = jnp.bitwise_and(jnp.right_shift(me, shift), members - 1)
        swaps = [
            send(spread.at[level, 0], spread.at[level + 1, d], level + 1, d,
                 (jnp.bitwise_xor(me, d << shift), rep))
            for d in range(1, members)
        ]
        for c in swaps:
            c.start()
        for c in swaps:
            c.wait()
        spread[level + 1, 0] = spread[level, 0]
        total = spread[level + 1, mine]
        for i in range(1, members):
            total = total + spread[level + 1, jnp.bitwise_xor(mine, i)]
        spread[level + 1, 0] = total

    last = len(digits) + 1
    gathered[rep] = spread[last, 0]
    spreads = [
        send(spread.at[last, 0], gathered.at[rep], last + 1, j, (me, partner))
        for j, partner in enumerate(rep_partners, start=1)
    ]
    for c in spreads:
        c.start()
    for c in spreads:
        c.wait()
    for r in range(group):
        out_ref[pl.ds(r * piece, piece)] = gathered[r]


def finish(partial_sums, share_root, feature_slab, scaled_sums, weight):
    group = lax.axis_size("rep")
    bits = lax.axis_size("blk").bit_length() - 1
    digits = [(shift, min(3, bits - shift)) for shift in range(0, bits, 3)]
    slab_rows, width = partial_sums.shape
    share = slab_rows // group
    fan = feature_slab.shape[1]
    piece = fan // group
    vmem = pl.BlockSpec(memory_space=pltpu.VMEM)
    return pl.pallas_call(
        functools.partial(finish_kernel, group, digits),
        out_shape=(
            jax.ShapeDtypeStruct((share, weight.shape[0]), jnp.bfloat16),
            jax.ShapeDtypeStruct((fan, width), jnp.float32),
        ),
        in_specs=[vmem] * 5,
        out_specs=(vmem, vmem),
        scratch_shapes=[
            pltpu.VMEM((fan, width), jnp.float32),
            pltpu.VMEM((group, share, width), partial_sums.dtype),
            pltpu.VMEM((group, piece, width), jnp.float32),
            pltpu.VMEM((len(digits) + 2, 8, piece, width), jnp.float32),
            pltpu.VMEM((group, piece, width), jnp.float32),
            pltpu.SemaphoreType.DMA((2, len(digits) + 3, 8)),
        ],
        compiler_params=pltpu.CompilerParams(collective_id=1, has_side_effects=True),
    )(partial_sums, share_root[:, None], feature_slab, scaled_sums, weight.T)


def slot_kernel(slots, coords_ref, counts_ref, src_ref, words_ref, root_ref, out_ref, sums_ref,
                scaled_ref):
    s = pl.program_id(0)

    @pl.when(s == 0)
    def _():
        out_ref[...] = jnp.zeros_like(out_ref)

    shifts = lax.broadcasted_iota(jnp.int32, (1, 8, 1), 1)
    for k in range(slots):
        @pl.when(k < counts_ref[s])
        def _():
            p = coords_ref[s, 0, k]
            q = coords_ref[s, 1, k]
            picked = src_ref[0, pl.ds(pl.multiple_of(p * 128, 128), 128), :]
            words = words_ref[0, k]
            bits = jnp.bitwise_and(jnp.right_shift(words[:, None, :], shifts), 1)
            transposed = bits.reshape(128, 128).astype(jnp.bfloat16)
            rows = pl.ds(pl.multiple_of(q * 128, 128), 128)
            out_ref[rows, :] += jnp.dot(transposed, picked, preferred_element_type=jnp.float32)

    @pl.when(s == pl.num_programs(0) - 1)
    def _():
        sums_ref[...] = out_ref[...].astype(sums_ref.dtype)
        scaled_ref[...] = (out_ref[...] * root_ref[...]).astype(scaled_ref.dtype)


def slot_sums(sources, words, coords, counts, inverse_root):
    steps, slab_rows, width = sources.shape
    slots = words.shape[1]
    grid_spec = pltpu.PrefetchScalarGridSpec(
        num_scalar_prefetch=2,
        grid=(steps,),
        in_specs=[
            pl.BlockSpec((1, slab_rows, width), lambda s, c, n: (s, 0, 0)),
            pl.BlockSpec((1,) + words.shape[1:], lambda s, c, n: (s, 0, 0, 0)),
            pl.BlockSpec((slab_rows, 1), lambda s, c, n: (0, 0)),
        ],
        out_specs=[
            pl.BlockSpec((slab_rows, width), lambda s, c, n: (0, 0)),
            pl.BlockSpec((slab_rows, width), lambda s, c, n: (0, 0)),
            pl.BlockSpec((slab_rows, width), lambda s, c, n: (0, 0)),
        ],
    )
    _, sums, scaled_sums = pl.pallas_call(
        functools.partial(slot_kernel, slots),
        out_shape=[
            jax.ShapeDtypeStruct((slab_rows, width), jnp.float32),
            jax.ShapeDtypeStruct((slab_rows, width), jnp.bfloat16),
            jax.ShapeDtypeStruct((slab_rows, width), jnp.bfloat16),
        ],
        grid_spec=grid_spec,
        compiler_params=pltpu.CompilerParams(dimension_semantics=("arbitrary",)),
    )(coords, counts, sources, words, inverse_root[:, None])
    return sums, scaled_sums


def per_device(features, out_grad, weight, block_words, block_coords, block_counts, degrees):
    slab_rows, width = out_grad.shape
    row_blocks = slab_rows // 128
    group_size = lax.axis_size("rep")
    blocks = lax.axis_size("blk")
    step_count = blocks // group_size
    rep_index = lax.axis_index("rep")
    inverse_root = lax.rsqrt(degrees.astype(jnp.float32))
    scaled = (out_grad.astype(jnp.float32) * inverse_root[:, None]).astype(jnp.bfloat16)

    sources, feature_slab = gather_sources(scaled, features, step_count, blocks, group_size)
    partial_sums, scaled_sums = slot_sums(
        sources, block_words[0], block_coords[0], block_counts[0], inverse_root
    )
    share_rows = slab_rows // group_size
    share_root = lax.dynamic_slice_in_dim(inverse_root, rep_index * share_rows, share_rows, 0)
    input_grad, weight_sum = finish(
        partial_sums, share_root, feature_slab.reshape(slab_rows, -1), scaled_sums, weight
    )
    node_total = slab_rows * blocks
    weight_grad = weight_sum * (1.0 / math.sqrt(node_total))
    return (input_grad, weight_grad)


def solution(mesh):
    return jax.shard_map(
        per_device,
        mesh=mesh,
        in_specs=(
            P(("blk", "rep"), None),
            P("blk", None),
            P(),
            P("blk", "rep", None, None, None),
            P("blk", "rep", None, None),
            P("blk", "rep"),
            P("blk"),
        ),
        out_specs=(P(("blk", "rep"), None), P()),
        check_vma=False,
    )
```

```python
import functools
import math

import jax
import jax.numpy as jnp
from jax import lax
from jax.experimental import pallas as pl
from jax.experimental.pallas import tpu as pltpu
from jax.sharding import PartitionSpec as P

CHUNKS = 16
MESH_ID = pl.DeviceIdType.MESH


def relay_plan(steps, blocks, group):
    plans = []
    for rep in range(group):
        reach = steps * rep + steps // 2
        short = min(reach, blocks - reach)
        if 16 * short < 3 * blocks:
            plans.append((CHUNKS, 0, 0))
            continue
        direct = min(CHUNKS, max(1, int(CHUNKS * (blocks - short) / blocks + 0.5)))
        sign = 1 if reach < blocks - reach else -1
        plans.append((direct, sign, (blocks - short) // 2))
    return plans


def gather_kernel(steps, blocks, plans, group, slab_ref, feat_ref, out_ref, feats_ref, relay_buf,
                  send_sem, recv_sem, relay_in_sem, relay_fwd_sem, feat_sem):
    me = lax.axis_index("blk")
    rep = lax.axis_index("rep")
    rows = slab_ref.shape[0] // CHUNKS
    centre = steps // 2
    reach = steps * rep + centre
    far_to = lax.rem(me - reach + blocks * steps, blocks)
    far_from = lax.rem(me + reach, blocks)
    left = lax.rem(me + blocks - 1, blocks)
    right = lax.rem(me + 1, blocks)

    def part(c):
        return pl.ds(c * rows, rows)

    def copy(src_slot, dst_slot, c, target):
        src = slab_ref.at[part(c)] if src_slot is None else out_ref.at[src_slot, part(c)]
        return pltpu.make_async_remote_copy(
            src_ref=src,
            dst_ref=out_ref.at[dst_slot, part(c)],
            send_sem=send_sem.at[dst_slot, c],
            recv_sem=recv_sem.at[dst_slot, c],
            device_id=(target, rep),
            device_id_type=MESH_ID,
        )

    def relay_out(c, target):
        return pltpu.make_async_remote_copy(
            src_ref=slab_ref.at[part(c)],
            dst_ref=relay_buf.at[c],
            send_sem=send_sem.at[centre, c],
            recv_sem=relay_in_sem.at[c],
            device_id=(target, rep),
            device_id_type=MESH_ID,
        )

    def relay_on(c, target):
        return pltpu.make_async_remote_copy(
            src_ref=relay_buf.at[c],
            dst_ref=out_ref.at[centre, part(c)],
            send_sem=relay_fwd_sem.at[c],
            recv_sem=recv_sem.at[centre, c],
            device_id=(target, rep),
            device_id_type=MESH_ID,
        )

    rep_partners = [lax.rem(rep + j, group) for j in range(1, group)]

    def feat_copy(j, partner):
        return pltpu.make_async_remote_copy(
            src_ref=feat_ref,
            dst_ref=feats_ref.at[rep],
            send_sem=feat_sem.at[0, j],
            recv_sem=feat_sem.at[1, j],
            device_id=(me, partner),
            device_id_type=MESH_ID,
        )

    barrier = pltpu.get_barrier_semaphore()
    for partner in (left, right, far_to, far_from):
        pl.semaphore_signal(barrier, inc=1, device_id=(partner, rep), device_id_type=MESH_ID)
    for partner in rep_partners:
        pl.semaphore_signal(barrier, inc=1, device_id=(me, partner), device_id_type=MESH_ID)
    own_feat = pltpu.make_async_copy(feat_ref, feats_ref.at[rep], feat_sem.at[0, 0])
    own_feat.start()

    for plane, (direct, sign, leg) in enumerate(plans):
        @pl.when(rep == plane)
        def _():
            if direct < CHUNKS:
                ahead = lax.rem(me + sign * leg + blocks, blocks)
                behind = lax.rem(me - sign * leg + blocks, blocks)
                for partner in (ahead, behind):
                    pl.semaphore_signal(barrier, inc=1, device_id=(partner, rep), device_id_type=MESH_ID)
                pl.semaphore_wait(barrier, 6 + group - 1)
                for c in range(direct):
                    copy(None, centre, c, far_to).start()
                for j, partner in enumerate(rep_partners, start=1):
                    feat_copy(j, partner).start()
                for c in range(direct, CHUNKS):
                    relay_out(c, ahead).start()
                for c in range(direct, CHUNKS):
                    relay_out(c, ahead).wait_recv()
                    relay_on(c, ahead).start()
            else:
                pl.semaphore_wait(barrier, 4 + group - 1)
                for c in range(CHUNKS):
                    copy(None, centre, c, far_to).start()
                for j, partner in enumerate(rep_partners, start=1):
                    feat_copy(j, partner).start()

    sent = []
    for k in range(1, centre + 1):
        for c in range(CHUNKS):
            up = centre + k
            down = centre - k
            if up < steps:
                copy(up - 1, up - 1, c, left).wait_recv()
                forward = copy(up - 1, up, c, left)
                forward.start()
                sent.append(forward)
            if down >= 0:
                if k > 1 or up >= steps:
                    copy(down + 1, down + 1, c, right).wait_recv()
                forward = copy(down + 1, down, c, right)
                forward.start()
                sent.append(forward)

    for c in range(CHUNKS):
        copy(None, steps - 1, c, left).wait_recv()
        copy(None, 0, c, right).wait_recv()

    for plane, (direct, sign, leg) in enumerate(plans):
        @pl.when(rep == plane)
        def _():
            ahead = lax.rem(me + sign * leg + blocks, blocks)
            for c in range(direct):
                copy(None, centre, c, far_to).wait_send()
            for c in range(direct, CHUNKS):
                relay_out(c, ahead).wait_send()
                relay_on(c, ahead).wait_send()
    for forward in sent:
        forward.wait_send()
    own_feat.wait()
    for j, partner in enumerate(rep_partners, start=1):
        feat_copy(j, partner).wait()


def gather_sources(scaled, features, steps, blocks, group):
    slab_rows, width = scaled.shape
    plans = relay_plan(steps, blocks, group)
    return pl.pallas_call(
        functools.partial(gather_kernel, steps, blocks, plans, group),
        out_shape=(
            jax.ShapeDtypeStruct((steps, slab_rows, width), scaled.dtype),
            jax.ShapeDtypeStruct((group,) + features.shape, features.dtype),
        ),
        in_specs=[pl.BlockSpec(memory_space=pl.ANY)] * 2,
        out_specs=(pl.BlockSpec(memory_space=pl.ANY), pl.BlockSpec(memory_space=pl.ANY)),
        scratch_shapes=[
            pltpu.VMEM((CHUNKS, slab_rows // CHUNKS, width), scaled.dtype),
            pltpu.SemaphoreType.DMA((steps, CHUNKS)),
            pltpu.SemaphoreType.DMA((steps, CHUNKS)),
            pltpu.SemaphoreType.DMA((CHUNKS,)),
            pltpu.SemaphoreType.DMA((CHUNKS,)),
            pltpu.SemaphoreType.DMA((2, group)),
        ],
        compiler_params=pltpu.CompilerParams(collective_id=0, has_side_effects=True),
    )(scaled, features)


def finish_kernel(group, digits, scale, partial_ref, root_ref, feat_ref, scaled_ref, weight_t_ref, grad_ref,
                  out_ref, term_ref, sums_in, inbox, spread, gathered, sems):
    me = lax.axis_index("blk")
    rep = lax.axis_index("rep")
    share = grad_ref.shape[0]
    piece = out_ref.shape[0] // group
    rep_partners = [lax.rem(rep + j, group) for j in range(1, group)]
    barrier = pltpu.get_barrier_semaphore()
    for partner in rep_partners:
        pl.semaphore_signal(barrier, inc=1, device_id=(me, partner), device_id_type=MESH_ID)
    blk_count = 0
    for shift, width in digits:
        for d in range(1, 1 << width):
            pl.semaphore_signal(
                barrier, inc=1, device_id=(jnp.bitwise_xor(me, d << shift), rep), device_id_type=MESH_ID
            )
            blk_count += 1
    term_ref[...] = lax.dot_general(
        feat_ref[...], scaled_ref[...], (((0,), (0,)), ((), ())), preferred_element_type=jnp.float32
    )
    pl.semaphore_wait(barrier, group - 1 + blk_count)

    def send(src, dst, sem_row, slot, device):
        return pltpu.make_async_remote_copy(
            src_ref=src,
            dst_ref=dst,
            send_sem=sems.at[0, sem_row, slot],
            recv_sem=sems.at[1, sem_row, slot],
            device_id=device,
            device_id_type=MESH_ID,
        )

    first = []
    for j, partner in enumerate(rep_partners, start=1):
        rows = pl.ds(pl.multiple_of(partner * share, 8), share)
        first.append(send(partial_ref.at[rows], sums_in.at[j], 0, j, (me, partner)))
        rows = pl.ds(pl.multiple_of(partner * piece, 8), piece)
        first.append(send(term_ref.at[rows], inbox.at[j], 1, j, (me, partner)))
    for c in first:
        c.start()
    for c in first:
        c.wait()
    own_rows = pl.ds(pl.multiple_of(rep * share, 8), share)
    summed = partial_ref[own_rows].astype(jnp.float32)
    for j in range(1, group):
        summed = summed + sums_in[j].astype(jnp.float32)
    aggregated = (summed * root_ref[...]).astype(jnp.bfloat16)
    grad_ref[...] = jnp.dot(
        aggregated, weight_t_ref[...], preferred_element_type=jnp.float32
    ).astype(grad_ref.dtype)
    own = pl.ds(pl.multiple_of(rep * piece, 8), piece)
    total = term_ref[own]
    for j in range(1, group):
        total = total + inbox[j]
    spread[1, 0] = total

    for level, (shift, width) in enumerate(digits, start=1):
        members = 1 << width
        mine = jnp.bitwise_and(jnp.right_shift(me, shift), members - 1)
        swaps = [
            send(spread.at[level, 0], spread.at[level + 1, d], level + 1, d,
                 (jnp.bitwise_xor(me, d << shift), rep))
            for d in range(1, members)
        ]
        for c in swaps:
            c.start()
        for c in swaps:
            c.wait()
        spread[level + 1, 0] = spread[level, 0]
        total = spread[level + 1, mine]
        for i in range(1, members):
            total = total + spread[level + 1, jnp.bitwise_xor(mine, i)]
        spread[level + 1, 0] = total

    last = len(digits) + 1
    gathered[rep] = spread[last, 0]
    spreads = [
        send(spread.at[last, 0], gathered.at[rep], last + 1, j, (me, partner))
        for j, partner in enumerate(rep_partners, start=1)
    ]
    for c in spreads:
        c.start()
    for c in spreads:
        c.wait()
    for r in range(group):
        out_ref[pl.ds(r * piece, piece)] = gathered[r] * scale


def finish(partial_sums, share_root, feature_slab, scaled_sums, weight, scale):
    group = lax.axis_size("rep")
    bits = lax.axis_size("blk").bit_length() - 1
    digits = [(shift, min(3, bits - shift)) for shift in range(0, bits, 3)]
    slab_rows, width = partial_sums.shape
    share = slab_rows // group
    fan = feature_slab.shape[1]
    piece = fan // group
    vmem = pl.BlockSpec(memory_space=pltpu.VMEM)
    return pl.pallas_call(
        functools.partial(finish_kernel, group, digits, scale),
        out_shape=(
            jax.ShapeDtypeStruct((share, weight.shape[0]), jnp.bfloat16),
            jax.ShapeDtypeStruct((fan, width), jnp.float32),
        ),
        in_specs=[vmem] * 5,
        out_specs=(vmem, vmem),
        scratch_shapes=[
            pltpu.VMEM((fan, width), jnp.float32),
            pltpu.VMEM((group, share, width), partial_sums.dtype),
            pltpu.VMEM((group, piece, width), jnp.float32),
            pltpu.VMEM((len(digits) + 2, 8, piece, width), jnp.float32),
            pltpu.VMEM((group, piece, width), jnp.float32),
            pltpu.SemaphoreType.DMA((2, len(digits) + 3, 8)),
        ],
        compiler_params=pltpu.CompilerParams(collective_id=1, has_side_effects=True),
    )(partial_sums, share_root[:, None], feature_slab, scaled_sums, weight.T)


def slot_kernel(slots, coords_ref, counts_ref, src_ref, words_ref, root_ref, out_ref, sums_ref,
                scaled_ref):
    s = pl.program_id(0)

    @pl.when(s == 0)
    def _():
        out_ref[...] = jnp.zeros_like(out_ref)

    shifts = lax.broadcasted_iota(jnp.int32, (1, 8, 1), 1)
    for k in range(slots):
        @pl.when(k < counts_ref[s])
        def _():
            p = coords_ref[s, 0, k]
            q = coords_ref[s, 1, k]
            picked = src_ref[0, pl.ds(pl.multiple_of(p * 128, 128), 128), :]
            words = words_ref[0, k]
            bits = jnp.bitwise_and(jnp.right_shift(words[:, None, :], shifts), 1)
            transposed = bits.reshape(128, 128).astype(jnp.bfloat16)
            rows = pl.ds(pl.multiple_of(q * 128, 128), 128)
            out_ref[rows, :] += jnp.dot(transposed, picked, preferred_element_type=jnp.float32)

    @pl.when(s == pl.num_programs(0) - 1)
    def _():
        sums_ref[...] = out_ref[...].astype(sums_ref.dtype)
        scaled_ref[...] = (out_ref[...] * root_ref[...]).astype(scaled_ref.dtype)


def slot_sums(sources, words, coords, counts, inverse_root):
    steps, slab_rows, width = sources.shape
    slots = words.shape[1]
    grid_spec = pltpu.PrefetchScalarGridSpec(
        num_scalar_prefetch=2,
        grid=(steps,),
        in_specs=[
            pl.BlockSpec((1, slab_rows, width), lambda s, c, n: (s, 0, 0)),
            pl.BlockSpec((1,) + words.shape[1:], lambda s, c, n: (s, 0, 0, 0)),
            pl.BlockSpec((slab_rows, 1), lambda s, c, n: (0, 0)),
        ],
        out_specs=[
            pl.BlockSpec((slab_rows, width), lambda s, c, n: (0, 0)),
            pl.BlockSpec((slab_rows, width), lambda s, c, n: (0, 0)),
            pl.BlockSpec((slab_rows, width), lambda s, c, n: (0, 0)),
        ],
    )
    _, sums, scaled_sums = pl.pallas_call(
        functools.partial(slot_kernel, slots),
        out_shape=[
            jax.ShapeDtypeStruct((slab_rows, width), jnp.float32),
            jax.ShapeDtypeStruct((slab_rows, width), jnp.bfloat16),
            jax.ShapeDtypeStruct((slab_rows, width), jnp.bfloat16),
        ],
        grid_spec=grid_spec,
        compiler_params=pltpu.CompilerParams(dimension_semantics=("arbitrary",)),
    )(coords, counts, sources, words, inverse_root[:, None])
    return sums, scaled_sums


def per_device(features, out_grad, weight, block_words, block_coords, block_counts, degrees):
    slab_rows, width = out_grad.shape
    row_blocks = slab_rows // 128
    group_size = lax.axis_size("rep")
    blocks = lax.axis_size("blk")
    step_count = blocks // group_size
    rep_index = lax.axis_index("rep")
    inverse_root = lax.rsqrt(degrees.astype(jnp.float32))
    scaled = (out_grad.astype(jnp.float32) * inverse_root[:, None]).astype(jnp.bfloat16)

    sources, feature_slab = gather_sources(scaled, features, step_count, blocks, group_size)
    partial_sums, scaled_sums = slot_sums(
        sources, block_words[0], block_coords[0], block_counts[0], inverse_root
    )
    share_rows = slab_rows // group_size
    share_root = lax.dynamic_slice_in_dim(inverse_root, rep_index * share_rows, share_rows, 0)
    node_total = slab_rows * blocks
    input_grad, weight_grad = finish(
        partial_sums, share_root, feature_slab.reshape(slab_rows, -1), scaled_sums, weight,
        1.0 / math.sqrt(node_total),
    )
    return (input_grad, weight_grad)


def solution(mesh):
    return jax.shard_map(
        per_device,
        mesh=mesh,
        in_specs=(
            P(("blk", "rep"), None),
            P("blk", None),
            P(),
            P("blk", "rep", None, None, None),
            P("blk", "rep", None, None),
            P("blk", "rep"),
            P("blk"),
        ),
        out_specs=(P(("blk", "rep"), None), P()),
        check_vma=False,
    )
```
